128 devices in a mesh: blk: 32 (over y_hi, x, z), sub: 4 (over y_lo, core).
Axes of the slice: x: 4, y: 4 (y_hi: 2, y_lo: 2; y = y_hi * 2 + y_lo), z: 4, core: 2. Of those that a mesh axis runs over, the one named last changes fastest.
Arguments:
- source: float32 [5, 32, 64, 8192], P(None, 'sub', None, 'blk'), may hold values from -30 to 30
- inv_diag: float32 [5, 32, 64, 8192], P(None, 'sub', None, 'blk'), may hold values from 0.1 to 0.25
- coupling: float32 [32, 6, 5, 5], P('blk'), may hold values from -0.6 to 0.6
- face_map: int32 [32, 2], replicated, may hold values from 0 to 31, as said below
- wall_jac: float32 [3, 5, 2, 32, 8192], P(None, None, None, 'sub', 'blk'), may hold values from -6 to 6
- ffd_weight: float32 [8, 32, 8192], P(None, 'sub', 'blk'), may hold values from 0.05 to 0.5
- cp_ids: int32 [8, 32, 8192], P(None, 'sub', 'blk'), may hold values from -1 to 49151, as said below
Outputs:
- adjoint: float32 [5, 32, 64, 8192], P(None, 'sub', None, 'blk')
- cp_sens: float32 [3, 49152], P(None, ('blk', 'sub'))
The draws below stay inside these ranges and needn't reach their ends.
Inputs may be any that keep to these rules, and one draw needn't show every extreme that they name: face_map[b, 0] is the block whose last chordwise cells meet block b's first ones; face_map[b, 1] the block whose first cells meet b's last ones; the second column is the inverse permutation of the first. `cp_ids`: -1 marks an unused slot; any other value is a control point, held by any device; the share of used slots differs from block to block.
All inputs are finite; a program needn't handle non-finite values.
Results may differ from the reference program's by a relative error of at most 0.0001.
Values sent between devices are 32-bit elements; how exact they have to be, the bound alone decides.
A program may use at most 192 MiB of HBM per device.

```python
import math
import jax
import jax.numpy as jnp
from jax import lax

NVAR = 5
CS = 8
CK = 64
CI = 256
SWEEPS = 3
STENCIL = 8
CP_DEV = 384
NBLK = 32
NS = 32
NI = 8192
NCP = 49152


def draw_face_map(key, part):
    order = jax.random.permutation(key, NBLK)
    inverse = jnp.argsort(order)
    return jnp.stack([order, inverse], 1).astype(jnp.int32)


def draw_cp_ids(key, part):
    key_points, key_level, key_slot, key_fixed = jax.random.split(key, 4)
    n_sub = NS // CS
    n_dev = NBLK * n_sub
    span_pos = jnp.arange(NS, dtype=jnp.int32)
    chord_pos = jnp.arange(NI, dtype=jnp.int32)
    holder = (chord_pos // CI)[None, :] * n_sub + (span_pos // CS)[:, None]
    points = jax.random.randint(key_points, (STENCIL, NS, NI), 0, NCP)
    level = jax.random.randint(key_level, (NBLK,), 2, 9)
    level_cols = jnp.repeat(level, CI)
    slot_draw = jax.random.randint(key_slot, (STENCIL, NS, NI), 0, 8)
    points = jnp.where(slot_draw < level_cols[None, None, :], points, -1)
    first_cell = ((span_pos % CS)[:, None] == 0) & ((chord_pos % CI)[None, :] == 0)
    fixed_off = jax.random.randint(key_fixed, (2, NS, NI), 0, CP_DEV)
    before = jnp.mod(holder - 1, n_dev) * CP_DEV + fixed_off[0]
    far = jnp.mod(holder + n_dev // 2, n_dev) * CP_DEV + fixed_off[1]
    points = points.at[0].set(jnp.where(first_cell, before, points[0]))
    points = points.at[1].set(jnp.where(first_cell, far, points[1]))
    points = points.at[0, NS - 1, NI - 1].set(NCP - 1).at[7, 0, 0].set(-1)
    return points.astype(jnp.int32)


def steps_of(own_key, dims, shards, low, top_value):
    def one(dim, parts):
        steps = jax.random.uniform(jax.random.fold_in(jax.random.fold_in(own_key, 6), dim), (parts,), jnp.float32, low / len(shards), top_value / len(shards))
        return jnp.repeat(jnp.exp(steps), dims[dim] // parts).reshape((-1,) + (1,) * (len(dims) - dim - 1))

    loudness = one(*shards[0])
    for cut in shards[1:]:
        loudness = loudness * one(*cut)
    return loudness


def centred(own_key, shape, spread, bound, shards=(), kind=jnp.bfloat16):
    array = spread * jax.random.normal(own_key, shape, jnp.float32)
    if shards:
        array = array * steps_of(own_key, shape, shards, -0.22, 0.18)
    return jnp.clip(array, -bound, bound).astype(kind)


def setup_inputs(seed: int = 0) -> dict:
    seeds = jax.random.split(jax.random.key(seed), 8)
    source = centred(seeds[0], (NVAR, NS, CK, NI), 5.0, 30.0, ((1, 4), (3, 32)), jnp.float32)
    inv_diag = jnp.clip(0.1 + 0.15 * jax.random.uniform(seeds[1], (NVAR, NS, CK, NI), jnp.float32) ** steps_of(seeds[1], (NVAR, NS, CK, NI), ((1, 4), (3, 32)), -0.2, 0.2), 0.1, 0.25)
    coupling = centred(seeds[2], (NBLK, 6, NVAR, NVAR), 0.12, 0.6, ((0, 32),), jnp.float32)
    face_map = draw_face_map(jax.random.fold_in(seeds[7], 71), 0)
    wall_jac = centred(seeds[4], (3, NVAR, 2, NS, NI), 1.0, 6.0, ((3, 4), (4, 32)), jnp.float32)
    ffd_weight = jnp.clip(jnp.exp(math.log(0.5) - 2.3025851 * jax.random.uniform(seeds[5], (STENCIL, NS, NI), jnp.float32) ** steps_of(seeds[5], (STENCIL, NS, NI), ((1, 4), (2, 32)), -0.2, 0.2)), 0.05, 0.5)
    cp_ids = draw_cp_ids(jax.random.fold_in(seeds[7], 71), 0)
    return {"source": source, "inv_diag": inv_diag, "coupling": coupling, "face_map": face_map, "wall_jac": wall_jac, "ffd_weight": ffd_weight, "cp_ids": cp_ids}


def couple_blocks(matrices, field):
    return jnp.einsum('buv,vsnbi->usnbi', matrices, field, precision=lax.Precision.HIGHEST)


def relax_field(adjoint, source, inv_diag, coupling, face_map):
    blocks = adjoint.reshape(NVAR, NS, CK, NBLK, CI)
    zero_span = jnp.zeros((NVAR, 1, CK, NBLK, CI), jnp.float32)
    zero_normal = jnp.zeros((NVAR, NS, 1, NBLK, CI), jnp.float32)
    span_low = jnp.concatenate([zero_span, blocks[:, :-1]], 1)
    span_high = jnp.concatenate([blocks[:, 1:], zero_span], 1)
    normal_low = jnp.concatenate([zero_normal, blocks[:, :, :-1]], 2)
    normal_high = jnp.concatenate([blocks[:, :, 1:], zero_normal], 2)
    last_cells = blocks[..., -1]
    first_cells = blocks[..., 0]
    low_face = jnp.take(last_cells, face_map[:, 0], axis=3)
    high_face = jnp.take(first_cells, face_map[:, 1], axis=3)
    chord_low = jnp.concatenate([low_face[..., None], blocks[..., :-1]], 4)
    chord_high = jnp.concatenate([blocks[..., 1:], high_face[..., None]], 4)
    summed = source.reshape(NVAR, NS, CK, NBLK, CI)
    neighbours = [span_low, span_high, normal_low, normal_high, chord_low, chord_high]
    for direction in range(6):
        summed = summed + couple_blocks(coupling[:, direction], neighbours[direction])
    return inv_diag * summed.reshape(NVAR, NS, CK, NI)


def reference(source, inv_diag, coupling, face_map, wall_jac, ffd_weight, cp_ids):
    adjoint = inv_diag * source
    for sweep_index in range(SWEEPS):
        adjoint = relax_field(adjoint, source, inv_diag, coupling, face_map)
    wall_sens = jnp.einsum('cvksi,vski->csi', wall_jac, adjoint[:, :, 0:2, :], precision=lax.Precision.HIGHEST)
    contrib = ffd_weight[None] * wall_sens[:, None]
    slots = jnp.where(cp_ids < 0, NCP, cp_ids).reshape(-1)

    def one_row(values):
        return jax.ops.segment_sum(values, slots, num_segments=NCP + 1)[:NCP]

    cp_sens = jax.vmap(one_row)(contrib.reshape(3, -1))
    return adjoint, cp_sens
```

```python
import functools

import jax
import jax.numpy as jnp
from jax import lax
from jax.experimental import pallas as pl
from jax.experimental.pallas import tpu as pltpu
from jax.sharding import PartitionSpec as P

MESH = pl.DeviceIdType.MESH
NVAR = 5
CS = 8
CK = 64
CI = 256
SWEEPS = 3
NBLK = 32
NSUB = 4
KT = CK // 8


def face_lane(half, tile, row):
    return half * 64 + tile * 8 + row


def place(lane, value, source_lane, target_lane, into):
    shift = lax.rem(target_lane - source_lane + 128, 128)
    return jnp.where(lane == target_lane, pltpu.roll(value, shift, 1), into)


def relax_row(s, p, q, q_pad, coup, src, invd, packed):
    row = lax.broadcasted_iota(jnp.int32, (8, CI), 0)
    lane = lax.broadcasted_iota(jnp.int32, (8, CI), 1)
    lane1 = lax.broadcasted_iota(jnp.int32, (8, 128), 1)
    zero = jnp.zeros((8, CI), jnp.float32)
    packed = list(packed)
    below = [zero] * NVAR
    here = [p[v, s + 1, 0:8, :] for v in range(NVAR)]
    here_up = [pltpu.roll(x, 7, 0) for x in here]
    for t in range(KT):
        rows = slice(8 * t, 8 * t + 8)
        if t < KT - 1:
            after = [p[v, s + 1, 8 * t + 8 : 8 * t + 16, :] for v in range(NVAR)]
            after_up = [pltpu.roll(x, 7, 0) for x in after]
        else:
            after, after_up = None, [zero] * NVAR
        acc = [src[u, s, rows, :] for u in range(NVAR)]
        for v in range(NVAR):
            x = here[v]
            down = pltpu.roll(x, 1, 0)
            nbs = (
                p[v, s, rows, :],
                p[v, s + 2, rows, :],
                jnp.where(row == 0, below[v], down),
                jnp.where(row == 7, after_up[v], here_up[v]),
                jnp.where(lane == 0, 0.0, pltpu.roll(x, 1, 1)),
                jnp.where(lane == CI - 1, 0.0, pltpu.roll(x, CI - 1, 1)),
            )
            below[v] = down
            for d in range(6):
                for u in range(NVAR):
                    acc[u] = acc[u] + coup[d * 25 + u * 5 + v] * nbs[d]
        for u in range(NVAR):
            value = invd[u, s, rows, :] * acc[u]
            q[u, s + q_pad, rows, :] = value
            if packed:
                both = place(lane1, value[:, 128:], 127, face_lane(0, t, s), packed[u])
                packed[u] = place(lane1, value[:, :128], 0, face_lane(1, t, s), both)
        here, here_up = after, after_up
    return tuple(packed)


def sweep_kernel(coup, fmap, src, invd, wjac, out, wall, p0, p1, p2, fsend, fbuf0, fbuf1, fbuf2, fs_sem, fr_sem, hs_sem, hr_sem):
    blk = lax.axis_index("blk")
    sub = lax.axis_index("sub")
    lane1 = lax.broadcasted_iota(jnp.int32, (8, 128), 1)
    fields = (p0, p1, p2)
    fbufs = (fbuf0, fbuf1, fbuf2)

    barrier = pltpu.get_barrier_semaphore()

    def greet(d, c):
        pl.semaphore_signal(barrier, inc=1, device_id=(lax.rem(blk + d, NBLK), sub), device_id_type=MESH)
        return c

    lax.fori_loop(1, NBLK, greet, 0)
    for step in (1, 3):
        pl.semaphore_signal(barrier, inc=1, device_id=(blk, lax.rem(sub + step, NSUB)), device_id_type=MESH)

    def first_row(s, packed):
        face, diag = list(packed[:NVAR]), list(packed[NVAR:])
        for v in range(NVAR):
            for t in range(KT):
                rows = slice(8 * t, 8 * t + 8)
                inv = invd[v, s, rows, :]
                value = inv * src[v, s, rows, :]
                p0[v, s + 1, rows, :] = value
                face[v] = place(lane1, value[:, 128:], 127, face_lane(0, t, s), face[v])
                face[v] = place(lane1, value[:, :128], 0, face_lane(1, t, s), face[v])
                diag[v] = place(lane1, inv[:, :128], 0, face_lane(0, t, s), diag[v])
                diag[v] = place(lane1, inv[:, 128:], 127, face_lane(1, t, s), diag[v])
        return tuple(face + diag)

    none = jnp.zeros((8, 128), jnp.float32)
    packed = lax.fori_loop(0, CS, first_row, (none,) * (2 * NVAR))
    face, diag = packed[:NVAR], packed[NVAR:]

    @pl.when(sub == 0)
    def _():
        for p in fields:
            p[:, 0] = jnp.zeros((NVAR, CK, CI), jnp.float32)

    @pl.when(sub == NSUB - 1)
    def _():
        for p in fields:
            p[:, CS + 1] = jnp.zeros((NVAR, CK, CI), jnp.float32)

    pl.semaphore_wait(barrier, NBLK - 1 + 2)

    def up_copy(n):
        return pltpu.make_async_remote_copy(
            src_ref=fields[n].at[:, CS], dst_ref=fields[n].at[:, 0], send_sem=hs_sem.at[n, 0], recv_sem=hr_sem.at[n, 0],
            device_id=(blk, lax.rem(sub + 1, NSUB)), device_id_type=MESH)

    def down_copy(n):
        return pltpu.make_async_remote_copy(
            src_ref=fields[n].at[:, 1], dst_ref=fields[n].at[:, CS + 1], send_sem=hs_sem.at[n, 1], recv_sem=hr_sem.at[n, 1],
            device_id=(blk, lax.rem(sub + NSUB - 1, NSUB)), device_id_type=MESH)

    for n in range(SWEEPS):
        p = fields[n]
        fbuf = fbufs[n]
        last = n == SWEEPS - 1
        q, q_pad = (out, 0) if last else (fields[n + 1], 1)

        for v in range(NVAR):
            fsend[n, v] = face[v]
            fbuf[blk, v] = face[v]

        def send_face(d, c):
            target = lax.rem(blk + d, NBLK)
            pltpu.make_async_remote_copy(
                src_ref=fsend.at[n], dst_ref=fbuf.at[blk], send_sem=fs_sem.at[n], recv_sem=fr_sem.at[n],
                device_id=(target, sub), device_id_type=MESH).start()
            return c

        lax.fori_loop(1, NBLK, send_face, 0, unroll=31)

        if n > 0:
            def add_faces(s, c):
                for u in range(NVAR):
                    for t in range(KT):
                        rows = slice(8 * t, 8 * t + 8)
                        low = place(lane1, extra[u], face_lane(0, t, s), 0, 0.0)
                        high = place(lane1, extra[u], face_lane(1, t, s), 127, 0.0)
                        p[u, s + 1, rows, 0:128] = p[u, s + 1, rows, 0:128] + low
                        p[u, s + 1, rows, 128:256] = p[u, s + 1, rows, 128:256] + high
                return c

            lax.fori_loop(0, 2, lambda i, c: add_faces(i * (CS - 1), c), 0)
        pl.when(sub < NSUB - 1)(lambda: up_copy(n).start())
        pl.when(sub > 0)(lambda: down_copy(n).start())
        if n > 0:
            lax.fori_loop(1, CS - 1, add_faces, 0)

        faces0 = () if last else (none,) * NVAR
        step = lambda s, c: relax_row(s, p, q, q_pad, coup, src, invd, c)
        faces0 = lax.fori_loop(1, CS - 1, step, faces0)
        pl.when(sub > 0)(lambda: up_copy(n).wait_recv())
        pl.when(sub < NSUB - 1)(lambda: down_copy(n).wait_recv())
        faces0 = lax.fori_loop(0, 2, lambda i, c: step(i * (CS - 1), c), faces0)

        landed = fbuf.at[pl.ds(0, NBLK - 1)]
        pltpu.make_async_copy(landed, landed, fr_sem.at[n]).wait()
        low = fbuf[fmap[2 * blk]]
        high = fbuf[fmap[2 * blk + 1]]
        from_low = lane1 < 64
        outer = [jnp.where(from_low, low[v], high[v]) for v in range(NVAR)]
        extra = []
        for u in range(NVAR):
            total = none
            for v in range(NVAR):
                total = total + jnp.where(from_low, coup[100 + u * 5 + v], coup[125 + u * 5 + v]) * outer[v]
            extra.append(diag[u] * total)
        if not last:
            face = [faces0[u] + pltpu.roll(extra[u], 64, 1) for u in range(NVAR)]

    def add_last(s, c):
        for u in range(NVAR):
            for t in range(KT):
                rows = slice(8 * t, 8 * t + 8)
                low = place(lane1, extra[u], face_lane(0, t, s), 0, 0.0)
                high = place(lane1, extra[u], face_lane(1, t, s), 127, 0.0)
                out[u, s, rows, 0:128] = out[u, s, rows, 0:128] + low
                out[u, s, rows, 128:256] = out[u, s, rows, 128:256] + high
        return c

    lax.fori_loop(0, CS, add_last, 0)
    for c in range(3):
        total = jnp.zeros((CS, CI), jnp.float32)
        for v in range(NVAR):
            for k in range(2):
                total = total + wjac[c, v, k] * out[v, :, k, :]
        wall[c] = total

    for n in range(SWEEPS):
        pl.when(sub < NSUB - 1)(lambda n=n: up_copy(n).wait_send())
        pl.when(sub > 0)(lambda n=n: down_copy(n).wait_send())
        sent = fbufs[n].at[pl.ds(0, NBLK - 1)]
        pltpu.make_async_copy(sent, sent, fs_sem.at[n]).wait()


def sweeps(source, inv_diag, coupling, face_map, wall_jac):
    vmem = pl.BlockSpec(memory_space=pltpu.VMEM)
    smem = pl.BlockSpec(memory_space=pltpu.SMEM)
    return pl.pallas_call(
        sweep_kernel,
        out_shape=(
            jax.ShapeDtypeStruct((NVAR, CS, CK, CI), jnp.float32),
            jax.ShapeDtypeStruct((3, CS, CI), jnp.float32),
        ),
        in_specs=[smem, smem, vmem, vmem, vmem],
        out_specs=(vmem, vmem),
        scratch_shapes=[pltpu.VMEM((NVAR, CS + 2, CK, CI), jnp.float32)] * 3
        + [
            pltpu.VMEM((SWEEPS, NVAR, 8, 128), jnp.float32),
            pltpu.VMEM((NBLK, NVAR, 8, 128), jnp.float32),
            pltpu.VMEM((NBLK, NVAR, 8, 128), jnp.float32),
            pltpu.VMEM((NBLK, NVAR, 8, 128), jnp.float32),
            pltpu.SemaphoreType.DMA((SWEEPS,)),
            pltpu.SemaphoreType.DMA((SWEEPS,)),
            pltpu.SemaphoreType.DMA((SWEEPS, 2)),
            pltpu.SemaphoreType.DMA((SWEEPS, 2)),
        ],
        compiler_params=pltpu.CompilerParams(collective_id=0, has_side_effects=True, vmem_limit_bytes=44 << 20),
        name="sweeps",
    )(coupling.reshape(-1), face_map.reshape(-1), source, inv_diag, wall_jac)


SLOT_TILE = 2048


def scatter_kernel(wall, weight, ids, dense, onehot, spread):
    m = pl.program_id(0)

    point = ids[0]
    high = point >> 7
    holder = (high * 171) >> 9
    order = (holder & 1) * 64 + (holder >> 1)
    rank = jnp.where(point < 0, -1, (high - 3 * holder) * 128 + order)
    low = point & 127
    pieces = []
    for c in range(3):
        value = weight[0] * wall[c]
        top = value.astype(jnp.bfloat16).astype(jnp.float32)
        pieces.append(top)
        pieces.append(value - top)
    for s in range(CS):
        lanes = slice(s * CI, (s + 1) * CI)
        hit = lax.broadcasted_iota(jnp.int32, (384, CI), 0) == rank[s : s + 1, :]
        onehot[:, lanes] = jnp.where(hit, 1.0, 0.0).astype(jnp.bfloat16)
        match = lax.broadcasted_iota(jnp.int32, (128, CI), 0) == low[s : s + 1, :]
        for i in range(6):
            spread[i * 128 : (i + 1) * 128, lanes] = jnp.where(match, pieces[i][s : s + 1, :], 0.0).astype(jnp.bfloat16)
    for j in range(3):
        part = lax.dot_general(
            onehot[j * 128 : (j + 1) * 128, :], spread[...], (((1,), (1,)), ((), ())), preferred_element_type=jnp.float32)
        for c in range(3):
            total = part[:, c * 256 : c * 256 + 128] + part[:, c * 256 + 128 : c * 256 + 256]
            for g in range(16):
                at = pl.ds(g * 128 + c * 3 + j, 8, stride=16)
                piece = total[g * 8 : g * 8 + 8, :]

                @pl.when(m == 0)
                def _():
                    dense[at, :] = piece

                @pl.when(m > 0)
                def _():
                    dense[at, :] = dense[at, :] + piece


def scatter(wall, weight, ids):
    return pl.pallas_call(
        scatter_kernel,
        grid=(8,),
        out_shape=jax.ShapeDtypeStruct((2048, 128), jnp.float32),
        in_specs=[
            pl.BlockSpec((3, CS, CI), lambda m: (0, 0, 0)),
            pl.BlockSpec((1, CS, CI), lambda m: (m, 0, 0)),
            pl.BlockSpec((1, CS, CI), lambda m: (m, 0, 0)),
        ],
        out_specs=pl.BlockSpec((2048, 128), lambda m: (0, 0)),
        scratch_shapes=[pltpu.VMEM((384, SLOT_TILE), jnp.bfloat16), pltpu.VMEM((768, SLOT_TILE), jnp.bfloat16)],
        compiler_params=pltpu.CompilerParams(vmem_limit_bytes=40 << 20),
        name="scatter",
    )(wall, weight, ids)


def holder_kernel(dense, out, pair, mine, landing, sems, fs_sem, fr_sem):
    blk = lax.axis_index("blk")
    sub = lax.axis_index("sub")
    side, core = sub // 2, lax.rem(sub, 2)
    chip = blk * 2 + side

    def device(other):
        return (other // 2, lax.rem(other, 2) * 2 + core)

    partner = (blk, side * 2 + 1 - core)
    barrier = pltpu.get_barrier_semaphore()

    def greet(d, c):
        pl.semaphore_signal(barrier, inc=1, device_id=device(lax.rem(chip + d, 64)), device_id_type=MESH)
        return c

    lax.fori_loop(1, 64, greet, 0)
    pl.semaphore_signal(barrier, inc=1, device_id=partner, device_id_type=MESH)
    pl.semaphore_wait(barrier, 64)

    swap = pltpu.make_async_remote_copy(
        src_ref=dense.at[pl.ds((1 - core) * 64, 64)], dst_ref=pair, send_sem=sems.at[0], recv_sem=sems.at[1],
        device_id=partner, device_id_type=MESH)
    swap.start()
    swap.wait()

    def add(i, c):
        at = pl.ds(i * 8, 8)
        mine[at] = dense[pl.ds(core * 64 + i * 8, 8)] + pair[at]
        return c

    lax.fori_loop(0, 8, add, 0)

    def send(d, c):
        other = lax.rem(chip + d, 64)
        pltpu.make_async_remote_copy(
            src_ref=mine.at[other], dst_ref=landing.at[d], send_sem=fs_sem, recv_sem=fr_sem,
            device_id=device(other), device_id_type=MESH).start()
        return c

    lax.fori_loop(1, 64, send, 0, unroll=9)
    landing[0] = mine[chip]
    landed = landing.at[pl.ds(1, 63)]
    pltpu.make_async_copy(landed, landed, fr_sem).wait()

    def total(i, acc):
        return acc + landing[i]

    acc = lax.fori_loop(0, 64, total, jnp.zeros((16, 128), jnp.float32), unroll=8)
    for c in range(3):
        for j in range(3):
            out[c : c + 1, j * 128 : (j + 1) * 128] = acc[c * 3 + j : c * 3 + j + 1, :]
    pltpu.make_async_copy(landed, landed, fs_sem).wait()


def to_holders(dense):
    vmem = pl.BlockSpec(memory_space=pltpu.VMEM)
    return pl.pallas_call(
        holder_kernel,
        out_shape=jax.ShapeDtypeStruct((3, 384), jnp.float32),
        in_specs=[vmem],
        out_specs=vmem,
        scratch_shapes=[
            pltpu.VMEM((64, 16, 128), jnp.float32),
            pltpu.VMEM((64, 16, 128), jnp.float32),
            pltpu.VMEM((64, 16, 128), jnp.float32),
            pltpu.SemaphoreType.DMA((2,)),
            pltpu.SemaphoreType.DMA,
            pltpu.SemaphoreType.DMA,
        ],
        compiler_params=pltpu.CompilerParams(collective_id=1, has_side_effects=True),
        name="to_holders",
    )(dense.reshape(128, 16, 128))


def body(source, inv_diag, coupling, face_map, wall_jac, ffd_weight, cp_ids):
    adjoint, wall = sweeps(source, inv_diag, coupling[0], face_map, wall_jac)
    dense = scatter(wall, ffd_weight, cp_ids)
    return adjoint, to_holders(dense)


def solution(mesh):
    in_specs = (
        P(None, "sub", None, "blk"),
        P(None, "sub", None, "blk"),
        P("blk", None, None, None),
        P(),
        P(None, None, None, "sub", "blk"),
        P(None, "sub", "blk"),
        P(None, "sub", "blk"),
    )
    out_specs = (P(None, "sub", None, "blk"), P(None, ("blk", "sub")))
    return jax.shard_map(body, mesh=mesh, in_specs=in_specs, out_specs=out_specs, check_vma=False)
```

```python
import functools

import jax
import jax.numpy as jnp
from jax import lax
from jax.experimental import pallas as pl
from jax.experimental.pallas import tpu as pltpu
from jax.sharding import PartitionSpec as P

MESH = pl.DeviceIdType.MESH
NVAR = 5
CS = 8
CK = 64
CI = 256
SWEEPS = 3
NBLK = 32
NSUB = 4
KT = CK // 8
HALVES = (slice(0, 128), slice(128, 256))


def face_lane(half, tile, row):
    return half * 64 + tile * 8 + row


def place(lane, value, source_lane, target_lane, into):
    shift = lax.rem(target_lane - source_lane + 128, 128)
    return jnp.where(lane == target_lane, pltpu.roll(value, shift, 1), into)


def relax_row(s, p, q, q_pad, coef, src, invd, packed):
    row = lax.broadcasted_iota(jnp.int32, (8, 128), 0)
    lane = lax.broadcasted_iota(jnp.int32, (8, 128), 1)
    zero = jnp.zeros((8, 128), jnp.float32)
    packed = list(packed)
    below = [[zero, zero] for _ in range(NVAR)]
    here = [[p[v, s + 1, 0:8, h] for h in HALVES] for v in range(NVAR)]
    here_up = [[pltpu.roll(x, 7, 0) for x in pair] for pair in here]
    for t in range(KT):
        rows = slice(8 * t, 8 * t + 8)
        if t < KT - 1:
            after = [[p[v, s + 1, 8 * t + 8 : 8 * t + 16, h] for h in HALVES] for v in range(NVAR)]
            after_up = [[pltpu.roll(x, 7, 0) for x in pair] for pair in after]
        else:
            after, after_up = None, [[zero, zero]] * NVAR
        acc = [[src[u, s, rows, h] for h in HALVES] for u in range(NVAR)]
        for v in range(NVAR):
            x = here[v]
            down = [pltpu.roll(a, 1, 0) for a in x]
            right = [pltpu.roll(a, 1, 1) for a in x]
            left = [pltpu.roll(a, 127, 1) for a in x]
            nbs = (
                [p[v, s, rows, h] for h in HALVES],
                [p[v, s + 2, rows, h] for h in HALVES],
                [jnp.where(row == 0, a, b) for a, b in zip(below[v], down)],
                [jnp.where(row == 7, a, b) for a, b in zip(after_up[v], here_up[v])],
                [jnp.where(lane == 0, 0.0, right[0]), jnp.where(lane == 0, right[0], right[1])],
                [jnp.where(lane == 127, left[1], left[0]), jnp.where(lane == 127, 0.0, left[1])],
            )
            below[v] = down
            for d in range(6):
                for u in range(NVAR):
                    factor = coef[d * 25 + u * 5 + v]
                    for h in range(2):
                        acc[u][h] = acc[u][h] + factor * nbs[d][h]
        for u in range(NVAR):
            value = [invd[u, s, rows, HALVES[h]] * acc[u][h] for h in range(2)]
            for h in range(2):
                q[u, s + q_pad, rows, HALVES[h]] = value[h]
            if packed:
                both = place(lane, value[1], 127, face_lane(0, t, s), packed[u])
                packed[u] = place(lane, value[0], 0, face_lane(1, t, s), both)
        here, here_up = after, after_up
    return tuple(packed)


def kernel(coup, fmap, src_hbm, invd_hbm, wjac_hbm, weight_hbm, ids_hbm, out, sens, src, invd, wjac, weight, ids, coef,
           p0, p1, p2, fsend, fbuf0, fbuf1, fbuf2, wall, onehot, spread, acc, dense, pair, mine, landing,
           ld_sem, fs_sem, fr_sem, hs_sem, hr_sem, sw_sem, ds_sem, dr_sem):
    blk = lax.axis_index("blk")
    sub = lax.axis_index("sub")
    side, core = sub // 2, lax.rem(sub, 2)
    chip = blk * 2 + side
    lane1 = lax.broadcasted_iota(jnp.int32, (8, 128), 1)
    fields = (p0, p1, p2)
    fbufs = (fbuf0, fbuf1, fbuf2)

    def same_core(other):
        return (other // 2, lax.rem(other, 2) * 2 + core)

    loads = [
        pltpu.make_async_copy(a, b, ld_sem.at[i])
        for i, (a, b) in enumerate(((src_hbm, src), (invd_hbm, invd), (wjac_hbm, wjac), (weight_hbm, weight), (ids_hbm, ids)))
    ]
    for copy in loads:
        copy.start()

    barrier = pltpu.get_barrier_semaphore()

    def greet(d, c):
        pl.semaphore_signal(barrier, inc=1, device_id=same_core(lax.rem(chip + d, 64)), device_id_type=MESH)
        return c

    lax.fori_loop(1, 64, greet, 0)
    for step in (1, 3):
        pl.semaphore_signal(barrier, inc=1, device_id=(blk, lax.rem(sub + step, NSUB)), device_id_type=MESH)

    for d in range(6):
        for u in range(NVAR):
            for v in range(NVAR):
                coef[d * 25 + u * 5 + v] = jnp.full((8, 128), coup[0, d, u, v], jnp.float32)

    @pl.when(sub == 0)
    def _():
        for p in fields:
            p[:, 0] = jnp.zeros((NVAR, CK, CI), jnp.float32)

    @pl.when(sub == NSUB - 1)
    def _():
        for p in fields:
            p[:, CS + 1] = jnp.zeros((NVAR, CK, CI), jnp.float32)

    loads[0].wait()
    loads[1].wait()

    def first_row(s, packed):
        face, diag = list(packed[:NVAR]), list(packed[NVAR:])
        for v in range(NVAR):
            for t in range(KT):
                rows = slice(8 * t, 8 * t + 8)
                inv = invd[v, s, rows, :]
                value = inv * src[v, s, rows, :]
                p0[v, s + 1, rows, :] = value
                face[v] = place(lane1, value[:, 128:], 127, face_lane(0, t, s), face[v])
                face[v] = place(lane1, value[:, :128], 0, face_lane(1, t, s), face[v])
                diag[v] = place(lane1, inv[:, :128], 0, face_lane(0, t, s), diag[v])
                diag[v] = place(lane1, inv[:, 128:], 127, face_lane(1, t, s), diag[v])
        return tuple(face + diag)

    none = jnp.zeros((8, 128), jnp.float32)
    packed = lax.fori_loop(0, CS, first_row, (none,) * (2 * NVAR))
    face, diag = packed[:NVAR], packed[NVAR:]

    pl.semaphore_wait(barrier, 65)

    def up_copy(n):
        return pltpu.make_async_remote_copy(
            src_ref=fields[n].at[:, CS], dst_ref=fields[n].at[:, 0], send_sem=hs_sem.at[n, 0], recv_sem=hr_sem.at[n, 0],
            device_id=(blk, lax.rem(sub + 1, NSUB)), device_id_type=MESH)

    def down_copy(n):
        return pltpu.make_async_remote_copy(
            src_ref=fields[n].at[:, 1], dst_ref=fields[n].at[:, CS + 1], send_sem=hs_sem.at[n, 1], recv_sem=hr_sem.at[n, 1],
            device_id=(blk, lax.rem(sub + NSUB - 1, NSUB)), device_id_type=MESH)

    for n in range(SWEEPS):
        p = fields[n]
        fbuf = fbufs[n]
        last = n == SWEEPS - 1
        q, q_pad = (out, 0) if last else (fields[n + 1], 1)

        for v in range(NVAR):
            fsend[n, v] = face[v]
            fbuf[blk, v] = face[v]

        def send_face(d, c):
            target = lax.rem(blk + d, NBLK)
            pltpu.make_async_remote_copy(
                src_ref=fsend.at[n], dst_ref=fbuf.at[blk], send_sem=fs_sem.at[n], recv_sem=fr_sem.at[n],
                device_id=(target, sub), device_id_type=MESH).start()
            return c

        lax.fori_loop(1, NBLK, send_face, 0, unroll=31)

        if n > 0:
            def add_faces(s, c):
                for u in range(NVAR):
                    for t in range(KT):
                        rows = slice(8 * t, 8 * t + 8)
                        low = place(lane1, extra[u], face_lane(0, t, s), 0, 0.0)
                        high = place(lane1, extra[u], face_lane(1, t, s), 127, 0.0)
                        p[u, s + 1, rows, 0:128] = p[u, s + 1, rows, 0:128] + low
                        p[u, s + 1, rows, 128:256] = p[u, s + 1, rows, 128:256] + high
                return c

            lax.fori_loop(0, 2, lambda i, c: add_faces(i * (CS - 1), c), 0)
        pl.when(sub < NSUB - 1)(lambda: up_copy(n).start())
        pl.when(sub > 0)(lambda: down_copy(n).start())
        if n > 0:
            lax.fori_loop(1, CS - 1, add_faces, 0)

        faces0 = () if last else (none,) * NVAR
        step = lambda s, c: relax_row(s, p, q, q_pad, coef, src, invd, c)
        faces0 = lax.fori_loop(1, CS - 1, step, faces0)
        pl.when(sub > 0)(lambda: up_copy(n).wait_recv())
        pl.when(sub < NSUB - 1)(lambda: down_copy(n).wait_recv())
        faces0 = lax.fori_loop(0, 2, lambda i, c: step(i * (CS - 1), c), faces0)

        landed = fbuf.at[pl.ds(0, NBLK - 1)]
        pltpu.make_async_copy(landed, landed, fr_sem.at[n]).wait()
        low = fbuf[fmap[blk, 0]]
        high = fbuf[fmap[blk, 1]]
        from_low = lane1 < 64
        outer = [jnp.where(from_low, low[v], high[v]) for v in range(NVAR)]
        extra = []
        for u in range(NVAR):
            total = none
            for v in range(NVAR):
                total = total + jnp.where(from_low, coef[100 + u * 5 + v], coef[125 + u * 5 + v]) * outer[v]
            extra.append(diag[u] * total)
        if not last:
            face = [faces0[u] + pltpu.roll(extra[u], 64, 1) for u in range(NVAR)]

    def add_last(s, c):
        for u in range(NVAR):
            for t in range(KT):
                rows = slice(8 * t, 8 * t + 8)
                low = place(lane1, extra[u], face_lane(0, t, s), 0, 0.0)
                high = place(lane1, extra[u], face_lane(1, t, s), 127, 0.0)
                out[u, s, rows, 0:128] = out[u, s, rows, 0:128] + low
                out[u, s, rows, 128:256] = out[u, s, rows, 128:256] + high
        return c

    lax.fori_loop(0, CS, add_last, 0)
    for copy in loads[2:]:
        copy.wait()
    for c in range(3):
        total = jnp.zeros((CS, CI), jnp.float32)
        for v in range(NVAR):
            for k in range(2):
                total = total + wjac[c, v, k] * out[v, :, k, :]
        wall[c] = total

    acc[...] = jnp.zeros_like(acc)

    def slots(m, carry):
        point = ids[m]
        high = point >> 7
        holder = (high * 171) >> 9
        order = (holder & 1) * 64 + (holder >> 1)
        rank = jnp.where(point < 0, -1, (high - 3 * holder) * 128 + order)
        low = point & 127
        pieces = []
        for c in range(3):
            value = weight[m] * wall[c]
            top = value.astype(jnp.bfloat16).astype(jnp.float32)
            pieces.append(top)
            pieces.append(value - top)
        for s in range(CS):
            lanes = slice(s * CI, (s + 1) * CI)
            hit = lax.broadcasted_iota(jnp.int32, (384, CI), 0) == rank[s : s + 1, :]
            onehot[:, lanes] = jnp.where(hit, 1.0, 0.0).astype(jnp.bfloat16)
            match = lax.broadcasted_iota(jnp.int32, (128, CI), 0) == low[s : s + 1, :]
            for i in range(6):
                spread[i * 128 : (i + 1) * 128, lanes] = jnp.where(match, pieces[i][s : s + 1, :], 0.0).astype(jnp.bfloat16)
        acc[...] = acc[...] + lax.dot_general(
            onehot[...], spread[...], (((1,), (1,)), ((), ())), preferred_element_type=jnp.float32)
        return carry

    lax.fori_loop(0, 8, slots, 0)
    for j in range(3):
        for c in range(3):
            for g in range(16):
                rows = slice(j * 128 + g * 8, j * 128 + g * 8 + 8)
                total = acc[rows, c * 256 : c * 256 + 128] + acc[rows, c * 256 + 128 : c * 256 + 256]
                dense[pl.ds(g * 128 + c * 3 + j, 8, stride=16), :] = total

    swap = pltpu.make_async_remote_copy(
        src_ref=dense.at[pl.ds((1 - core) * 1024, 1024)], dst_ref=pair, send_sem=sw_sem.at[0], recv_sem=sw_sem.at[1],
        device_id=(blk, side * 2 + 1 - core), device_id_type=MESH)
    swap.start()
    swap.wait()

    def add(i, c):
        both = dense[pl.ds(core * 1024 + i * 16, 16), :] + pair[pl.ds(i * 16, 16), :]
        mine[i] = both[:9, :]
        return c

    lax.fori_loop(0, 64, add, 0, unroll=8)

    def send_points(d, c):
        other = lax.rem(chip + d, 64)
        pltpu.make_async_remote_copy(
            src_ref=mine.at[other], dst_ref=landing.at[d], send_sem=ds_sem, recv_sem=dr_sem,
            device_id=same_core(other), device_id_type=MESH).start()
        return c

    lax.fori_loop(1, 64, send_points, 0, unroll=9)
    landing[0] = mine[chip]
    landed = landing.at[pl.ds(1, 63)]
    pltpu.make_async_copy(landed, landed, dr_sem).wait()
    total = lax.fori_loop(0, 64, lambda i, t: t + landing[i], jnp.zeros((9, 128), jnp.float32), unroll=8)
    for c in range(3):
        for j in range(3):
            sens[c : c + 1, j * 128 : (j + 1) * 128] = total[c * 3 + j : c * 3 + j + 1, :]
    pltpu.make_async_copy(landed, landed, ds_sem).wait()

    for n in range(SWEEPS):
        pl.when(sub < NSUB - 1)(lambda n=n: up_copy(n).wait_send())
        pl.when(sub > 0)(lambda n=n: down_copy(n).wait_send())
        sent = fbufs[n].at[pl.ds(0, NBLK - 1)]
        pltpu.make_async_copy(sent, sent, fs_sem.at[n]).wait()


def body(source, inv_diag, coupling, face_map, wall_jac, ffd_weight, cp_ids):
    vmem = pl.BlockSpec(memory_space=pltpu.VMEM)
    smem = pl.BlockSpec(memory_space=pltpu.SMEM)
    hbm = pl.BlockSpec(memory_space=pl.ANY)
    f32, dma = jnp.float32, pltpu.SemaphoreType.DMA
    face_buffer = pltpu.VMEM((NBLK, NVAR, 8, 128), f32)
    field = pltpu.VMEM((NVAR, CS + 2, CK, CI), f32)
    return pl.pallas_call(
        kernel,
        out_shape=(jax.ShapeDtypeStruct((NVAR, CS, CK, CI), f32), jax.ShapeDtypeStruct((3, 384), f32)),
        in_specs=[smem, smem, hbm, hbm, hbm, hbm, hbm],
        out_specs=(vmem, vmem),
        scratch_shapes=[
            pltpu.VMEM((NVAR, CS, CK, CI), f32),
            pltpu.VMEM((NVAR, CS, CK, CI), f32),
            pltpu.VMEM((3, NVAR, 2, CS, CI), f32),
            pltpu.VMEM((8, CS, CI), f32),
            pltpu.VMEM((8, CS, CI), jnp.int32),
            pltpu.VMEM((150, 8, 128), f32),
            field,
            field,
            field,
            pltpu.VMEM((SWEEPS, NVAR, 8, 128), f32),
            face_buffer,
            face_buffer,
            face_buffer,
            pltpu.VMEM((3, CS, CI), f32),
            pltpu.VMEM((384, CS * CI), jnp.bfloat16),
            pltpu.VMEM((768, CS * CI), jnp.bfloat16),
            pltpu.VMEM((384, 768), f32),
            pltpu.VMEM((2048, 128), f32),
            pltpu.VMEM((1024, 128), f32),
            pltpu.VMEM((64, 9, 128), f32),
            pltpu.VMEM((64, 9, 128), f32),
            dma((5,)),
            dma((SWEEPS,)),
            dma((SWEEPS,)),
            dma((SWEEPS, 2)),
            dma((SWEEPS, 2)),
            dma((2,)),
            dma,
            dma,
        ],
        compiler_params=pltpu.CompilerParams(collective_id=0, has_side_effects=True, vmem_limit_bytes=56 << 20),
        name="adjoint",
    )(coupling, face_map, source, inv_diag, wall_jac, ffd_weight, cp_ids)


def solution(mesh):
    in_specs = (
        P(None, "sub", None, "blk"),
        P(None, "sub", None, "blk"),
        P("blk", None, None, None),
        P(),
        P(None, None, None, "sub", "blk"),
        P(None, "sub", "blk"),
        P(None, "sub", "blk"),
    )
    out_specs = (P(None, "sub", None, "blk"), P(None, ("blk", "sub")))
    return jax.shard_map(body, mesh=mesh, in_specs=in_specs, out_specs=out_specs, check_vma=False)
```

```python
import functools

import jax
import jax.numpy as jnp
from jax import lax
from jax.experimental import pallas as pl
from jax.experimental.pallas import tpu as pltpu
from jax.sharding import PartitionSpec as P

MESH = pl.DeviceIdType.MESH
NVAR = 5
CS = 8
CK = 64
CI = 256
SWEEPS = 3
NBLK = 32
NSUB = 4
KT = CK // 8
SPAN_ROWS = ((0, 8), (8, CK - 8))
HALVES = (slice(0, 128), slice(128, 256))


def face_lane(half, tile, row):
    return half * 64 + tile * 8 + row


def place(lane, value, source_lane, target_lane, into):
    shift = lax.rem(target_lane - source_lane + 128, 128)
    return jnp.where(lane == target_lane, pltpu.roll(value, shift, 1), into)


def relax_row(s, p, q, q_pad, coef, src, invd, packed, first=0, end=KT):
    row = lax.broadcasted_iota(jnp.int32, (8, 128), 0)
    lane = lax.broadcasted_iota(jnp.int32, (8, 128), 1)
    zero = jnp.zeros((8, 128), jnp.float32)
    packed = list(packed)
    if first:
        edge = slice(8 * first - 8, 8 * first)
        below = [[pltpu.roll(p[v, s + 1, edge, h], 1, 0) for h in HALVES] for v in range(NVAR)]
    else:
        below = [[zero, zero] for _ in range(NVAR)]
    here = [[p[v, s + 1, 8 * first : 8 * first + 8, h] for h in HALVES] for v in range(NVAR)]
    here_up = [[pltpu.roll(x, 7, 0) for x in pair] for pair in here]
    for t in range(first, end):
        rows = slice(8 * t, 8 * t + 8)
        if t < KT - 1:
            after = [[p[v, s + 1, 8 * t + 8 : 8 * t + 16, h] for h in HALVES] for v in range(NVAR)]
            after_up = [[pltpu.roll(x, 7, 0) for x in pair] for pair in after]
        else:
            after, after_up = None, [[zero, zero]] * NVAR
        acc = [[src[u, s, rows, h] for h in HALVES] for u in range(NVAR)]
        for v in range(NVAR):
            x = here[v]
            down = [pltpu.roll(a, 1, 0) for a in x]
            right = [pltpu.roll(a, 1, 1) for a in x]
            left = [pltpu.roll(a, 127, 1) for a in x]
            nbs = (
                [p[v, s, rows, h] for h in HALVES],
                [p[v, s + 2, rows, h] for h in HALVES],
                [jnp.where(row == 0, a, b) for a, b in zip(below[v], down)],
                [jnp.where(row == 7, a, b) for a, b in zip(after_up[v], here_up[v])],
                [jnp.where(lane == 0, 0.0, right[0]), jnp.where(lane == 0, right[0], right[1])],
                [jnp.where(lane == 127, left[1], left[0]), jnp.where(lane == 127, 0.0, left[1])],
            )
            below[v] = down
            for d in range(6):
                for u in range(NVAR):
                    factor = coef[d * 25 + u * 5 + v]
                    for h in range(2):
                        acc[u][h] = acc[u][h] + factor * nbs[d][h]
        for u in range(NVAR):
            value = [invd[u, s, rows, HALVES[h]] * acc[u][h] for h in range(2)]
            for h in range(2):
                q[u, s + q_pad, rows, HALVES[h]] = value[h]
            if packed:
                both = place(lane, value[1], 127, face_lane(0, t, s), packed[u])
                packed[u] = place(lane, value[0], 0, face_lane(1, t, s), both)
        here, here_up = after, after_up
    return tuple(packed)


def kernel(coup, fmap, src_hbm, invd_hbm, wjac_hbm, weight_hbm, ids_hbm, out, sens, src, invd, wjac, weight, ids, coef,
           p0, p1, p2, fsend, fbuf0, fbuf1, fbuf2, wall, onehot, spread, acc, dense, pair, mine, landing,
           ld_sem, fs_sem, fr_sem, hs_sem, hr_sem, sw_sem, ds_sem, dr_sem):
    blk = lax.axis_index("blk")
    sub = lax.axis_index("sub")
    side, core = sub // 2, lax.rem(sub, 2)
    chip = blk * 2 + side
    lane1 = lax.broadcasted_iota(jnp.int32, (8, 128), 1)
    fields = (p0, p1, p2)
    fbufs = (fbuf0, fbuf1, fbuf2)

    def same_core(other):
        return (other // 2, lax.rem(other, 2) * 2 + core)

    loads = [
        pltpu.make_async_copy(a, b, ld_sem.at[i])
        for i, (a, b) in enumerate(((src_hbm, src), (invd_hbm, invd), (wjac_hbm, wjac), (weight_hbm, weight), (ids_hbm, ids)))
    ]
    for copy in loads:
        copy.start()

    barrier = pltpu.get_barrier_semaphore()

    def greet(d, c):
        pl.semaphore_signal(barrier, inc=1, device_id=same_core(lax.rem(chip + d, 64)), device_id_type=MESH)
        return c

    lax.fori_loop(1, 64, greet, 0)
    for step in (1, 3):
        pl.semaphore_signal(barrier, inc=1, device_id=(blk, lax.rem(sub + step, NSUB)), device_id_type=MESH)

    for d in range(6):
        for u in range(NVAR):
            for v in range(NVAR):
                coef[d * 25 + u * 5 + v] = jnp.full((8, 128), coup[u, v, 0, d], jnp.float32)

    @pl.when(sub == 0)
    def _():
        for p in fields:
            p[:, 0] = jnp.zeros((NVAR, CK, CI), jnp.float32)

    @pl.when(sub == NSUB - 1)
    def _():
        for p in fields:
            p[:, CS + 1] = jnp.zeros((NVAR, CK, CI), jnp.float32)

    loads[0].wait()
    loads[1].wait()

    def first_row(s, packed):
        face, diag = list(packed[:NVAR]), list(packed[NVAR:])
        for v in range(NVAR):
            for t in range(KT):
                rows = slice(8 * t, 8 * t + 8)
                inv = invd[v, s, rows, :]
                value = inv * src[v, s, rows, :]
                p0[v, s + 1, rows, :] = value
                face[v] = place(lane1, value[:, 128:], 127, face_lane(0, t, s), face[v])
                face[v] = place(lane1, value[:, :128], 0, face_lane(1, t, s), face[v])
                diag[v] = place(lane1, inv[:, :128], 0, face_lane(0, t, s), diag[v])
                diag[v] = place(lane1, inv[:, 128:], 127, face_lane(1, t, s), diag[v])
        return tuple(face + diag)

    none = jnp.zeros((8, 128), jnp.float32)
    packed = lax.fori_loop(0, CS, first_row, (none,) * (2 * NVAR))
    face, diag = packed[:NVAR], packed[NVAR:]

    pl.semaphore_wait(barrier, 65)

    def up_copy(n, i):
        rows = pl.ds(*SPAN_ROWS[i])
        return pltpu.make_async_remote_copy(
            src_ref=fields[n].at[:, CS, rows], dst_ref=fields[n].at[:, 0, rows],
            send_sem=hs_sem.at[n, 0, i], recv_sem=hr_sem.at[n, 0, i],
            device_id=(blk, lax.rem(sub + 1, NSUB)), device_id_type=MESH)

    def down_copy(n, i):
        rows = pl.ds(*SPAN_ROWS[i])
        return pltpu.make_async_remote_copy(
            src_ref=fields[n].at[:, 1, rows], dst_ref=fields[n].at[:, CS + 1, rows],
            send_sem=hs_sem.at[n, 1, i], recv_sem=hr_sem.at[n, 1, i],
            device_id=(blk, lax.rem(sub + NSUB - 1, NSUB)), device_id_type=MESH)

    def start_spans(n):
        for i in range(2):
            pl.when(sub < NSUB - 1)(lambda: up_copy(n, i).start())
            pl.when(sub > 0)(lambda: down_copy(n, i).start())

    def spans_landed(n, i):
        pl.when(sub > 0)(lambda: up_copy(n, i).wait_recv())
        pl.when(sub < NSUB - 1)(lambda: down_copy(n, i).wait_recv())

    def send_faces(n):
        for v in range(NVAR):
            fsend[n, v] = face[v]
            fbufs[n][blk, v] = face[v]

        def send_face(d, c):
            target = lax.rem(blk + d, NBLK)
            pltpu.make_async_remote_copy(
                src_ref=fsend.at[n], dst_ref=fbufs[n].at[blk], send_sem=fs_sem.at[n], recv_sem=fr_sem.at[n],
                device_id=(target, sub), device_id_type=MESH).start()
            return c

        lax.fori_loop(1, NBLK, send_face, 0, unroll=31)

    def faces_landed(n):
        fbuf = fbufs[n]
        landed = fbuf.at[pl.ds(0, NBLK - 1)]
        pltpu.make_async_copy(landed, landed, fr_sem.at[n]).wait()
        low = fbuf[fmap[0, blk]]
        high = fbuf[fmap[1, blk]]
        from_low = lane1 < 64
        outer = [jnp.where(from_low, low[v], high[v]) for v in range(NVAR)]
        terms = []
        for u in range(NVAR):
            total = none
            for v in range(NVAR):
                total = total + jnp.where(from_low, coef[100 + u * 5 + v], coef[125 + u * 5 + v]) * outer[v]
            terms.append(diag[u] * total)
        return terms

    def add_faces(p, pad, s, terms, tiles=(0, KT)):
        for u in range(NVAR):
            for t in range(*tiles):
                rows = slice(8 * t, 8 * t + 8)
                low = place(lane1, terms[u], face_lane(0, t, s), 0, 0.0)
                high = place(lane1, terms[u], face_lane(1, t, s), 127, 0.0)
                p[u, s + pad, rows, 0:128] = p[u, s + pad, rows, 0:128] + low
                p[u, s + pad, rows, 128:256] = p[u, s + pad, rows, 128:256] + high

    def over(rows, step):
        lo, hi = rows
        lax.fori_loop(lo, hi, lambda s, c: (step(s), c)[1], 0)

    def ends(step):
        lax.fori_loop(0, 2, lambda i, c: (step(i * (CS - 1)), c)[1], 0)

    for n in range(SWEEPS - 1):
        p, q = fields[n], fields[n + 1]
        send_faces(n)
        if n > 0:
            ends(lambda s: add_faces(p, 1, s, extra))
        start_spans(n)
        if n > 0:
            over((1, CS - 1), lambda s: add_faces(p, 1, s, extra))
        step = lambda s, c: relax_row(s, p, q, 1, coef, src, invd, c)
        made = lax.fori_loop(1, CS - 1, step, (none,) * NVAR)
        spans_landed(n, 0)
        spans_landed(n, 1)
        made = lax.fori_loop(0, 2, lambda i, c: step(i * (CS - 1), c), made)
        extra = faces_landed(n)
        face = [made[u] + pltpu.roll(extra[u], 64, 1) for u in range(NVAR)]

    n = SWEEPS - 1
    p = fields[n]
    send_faces(n)
    ends(lambda s: add_faces(p, 1, s, extra))
    start_spans(n)
    over((1, CS - 1), lambda s: add_faces(p, 1, s, extra))

    def last_rows(s, first, end):
        relax_row(s, p, out, 0, coef, src, invd, (), first, end)

    over((1, CS - 1), lambda s: last_rows(s, 0, 1))
    over((1, 3), lambda s: last_rows(s, 1, KT))
    spans_landed(n, 0)
    ends(lambda s: last_rows(s, 0, 1))
    for copy in loads[2:]:
        copy.wait()

    def wall_of(c):
        total = jnp.zeros((CS, CI), jnp.float32)
        for v in range(NVAR):
            for k in range(2):
                total = total + wjac[c, v, k] * out[v, :, k, :]
        return total

    column = lax.broadcasted_iota(jnp.int32, (CS, CI), 1)
    inner = (column > 0) & (column < CI - 1)
    for c in range(3):
        wall[c] = jnp.where(inner, wall_of(c), 0.0)

    acc[...] = jnp.zeros_like(acc)

    def row_and_lane(point):
        high = point >> 7
        holder = (high * 171) >> 9
        order = (holder & 1) * 64 + (holder >> 1)
        return jnp.where(point < 0, -1, (high - 3 * holder) * 128 + order), point & 127

    def slots(m, carry):
        rank, low = row_and_lane(ids[m])
        pieces = []
        for c in range(3):
            value = weight[m] * wall[c]
            top = value.astype(jnp.bfloat16).astype(jnp.float32)
            pieces.append(top)
            pieces.append(value - top)
        for s in range(CS):
            lanes = slice(s * CI, (s + 1) * CI)
            hit = lax.broadcasted_iota(jnp.int32, (384, CI), 0) == rank[s : s + 1, :]
            onehot[:, lanes] = jnp.where(hit, 1.0, 0.0).astype(jnp.bfloat16)
            match = lax.broadcasted_iota(jnp.int32, (128, CI), 0) == low[s : s + 1, :]
            for i in range(6):
                spread[i * 128 : (i + 1) * 128, lanes] = jnp.where(match, pieces[i][s : s + 1, :], 0.0).astype(jnp.bfloat16)
        acc[...] = acc[...] + lax.dot_general(
            onehot[...], spread[...], (((1,), (1,)), ((), ())), preferred_element_type=jnp.float32)
        return carry

    lax.fori_loop(0, 8, slots, 0)

    extra = faces_landed(n)
    over((0, CS), lambda s: add_faces(out, 0, s, extra, (0, 1)))
    walls = [wall_of(c) for c in range(3)]
    marks = [jnp.full((8, 128), -1, jnp.int32), jnp.zeros((8, 128), jnp.int32)] + [none] * 3
    for m in range(8):
        rank, low = row_and_lane(ids[m])
        for i, x in enumerate([rank, low] + [weight[m] * walls[c] for c in range(3)]):
            marks[i] = place(lane1, x[:, :128], 0, 2 * m, marks[i])
            marks[i] = place(lane1, x[:, 128:], 127, 2 * m + 1, marks[i])
    line = lax.broadcasted_iota(jnp.int32, (1, 128), 1)
    flat = []
    for x in marks:
        total = x[0:1, :]
        for s in range(1, CS):
            total = jnp.where((line >> 4) == s, pltpu.roll(x[s : s + 1, :], 16 * s, 1), total)
        flat.append(total)
    hit = lax.broadcasted_iota(jnp.int32, (384, 128), 0) == flat[0]
    match = lax.broadcasted_iota(jnp.int32, (128, 128), 0) == flat[1]
    edge_spread = []
    for c in range(3):
        top = flat[2 + c].astype(jnp.bfloat16).astype(jnp.float32)
        for value in (top, flat[2 + c] - top):
            edge_spread.append(jnp.where(match, value, 0.0).astype(jnp.bfloat16))
    acc[...] = acc[...] + lax.dot_general(
        jnp.where(hit, 1.0, 0.0).astype(jnp.bfloat16), jnp.concatenate(edge_spread, 0), (((1,), (1,)), ((), ())),
        preferred_element_type=jnp.float32)
    for j in range(3):
        for c in range(3):
            for g in range(16):
                rows = slice(j * 128 + g * 8, j * 128 + g * 8 + 8)
                total = acc[rows, c * 256 : c * 256 + 128] + acc[rows, c * 256 + 128 : c * 256 + 256]
                dense[pl.ds(g * 128 + c * 3 + j, 8, stride=16), :] = total

    swap = pltpu.make_async_remote_copy(
        src_ref=dense.at[pl.ds((1 - core) * 1024, 1024)], dst_ref=pair, send_sem=sw_sem.at[0], recv_sem=sw_sem.at[1],
        device_id=(blk, side * 2 + 1 - core), device_id_type=MESH)
    swap.start()
    swap.wait()

    def add(i, c):
        both = dense[pl.ds(core * 1024 + i * 16, 16), :] + pair[pl.ds(i * 16, 16), :]
        mine[i] = both[:9, :]
        return c

    lax.fori_loop(0, 64, add, 0, unroll=8)

    def send_points(d, c):
        other = lax.rem(chip + d, 64)
        pltpu.make_async_remote_copy(
            src_ref=mine.at[other], dst_ref=landing.at[d], send_sem=ds_sem, recv_sem=dr_sem,
            device_id=same_core(other), device_id_type=MESH).start()
        return c

    lax.fori_loop(1, 64, send_points, 0, unroll=9)
    landing[0] = mine[chip]

    spans_landed(n, 1)
    over((3, CS - 1), lambda s: last_rows(s, 1, KT))
    ends(lambda s: last_rows(s, 1, KT))
    over((0, CS), lambda s: add_faces(out, 0, s, extra, (1, KT)))

    landed = landing.at[pl.ds(1, 63)]
    pltpu.make_async_copy(landed, landed, dr_sem).wait()
    total = lax.fori_loop(0, 64, lambda i, t: t + landing[i], jnp.zeros((9, 128), jnp.float32), unroll=8)
    for c in range(3):
        for j in range(3):
            sens[c : c + 1, j * 128 : (j + 1) * 128] = total[c * 3 + j : c * 3 + j + 1, :]
    pltpu.make_async_copy(landed, landed, ds_sem).wait()

    for n in range(SWEEPS):
        for i in range(2):
            pl.when(sub < NSUB - 1)(lambda: up_copy(n, i).wait_send())
            pl.when(sub > 0)(lambda: down_copy(n, i).wait_send())
        sent = fbufs[n].at[pl.ds(0, NBLK - 1)]
        pltpu.make_async_copy(sent, sent, fs_sem.at[n]).wait()


def body(source, inv_diag, coupling, face_map, wall_jac, ffd_weight, cp_ids):
    vmem = pl.BlockSpec(memory_space=pltpu.VMEM)
    smem = pl.BlockSpec(memory_space=pltpu.SMEM)
    hbm = pl.BlockSpec(memory_space=pltpu.HBM)
    f32, dma = jnp.float32, pltpu.SemaphoreType.DMA
    face_buffer = pltpu.VMEM((NBLK, NVAR, 8, 128), f32)
    field = pltpu.VMEM((NVAR, CS + 2, CK, CI), f32)
    return pl.pallas_call(
        kernel,
        out_shape=(jax.ShapeDtypeStruct((NVAR, CS, CK, CI), f32), jax.ShapeDtypeStruct((3, 384), f32)),
        in_specs=[smem, smem, hbm, hbm, hbm, hbm, hbm],
        out_specs=(vmem, vmem),
        scratch_shapes=[
            pltpu.VMEM((NVAR, CS, CK, CI), f32),
            pltpu.VMEM((NVAR, CS, CK, CI), f32),
            pltpu.VMEM((3, NVAR, 2, CS, CI), f32),
            pltpu.VMEM((8, CS, CI), f32),
            pltpu.VMEM((8, CS, CI), jnp.int32),
            pltpu.VMEM((150, 8, 128), f32),
            field,
            field,
            field,
            pltpu.VMEM((SWEEPS, NVAR, 8, 128), f32),
            face_buffer,
            face_buffer,
            face_buffer,
            pltpu.VMEM((3, CS, CI), f32),
            pltpu.VMEM((384, CS * CI), jnp.bfloat16),
            pltpu.VMEM((768, CS * CI), jnp.bfloat16),
            pltpu.VMEM((384, 768), f32),
            pltpu.VMEM((2048, 128), f32),
            pltpu.VMEM((1024, 128), f32),
            pltpu.VMEM((64, 9, 128), f32),
            pltpu.VMEM((64, 9, 128), f32),
            dma((5,)),
            dma((SWEEPS,)),
            dma((SWEEPS,)),
            dma((SWEEPS, 2, 2)),
            dma((SWEEPS, 2, 2)),
            dma((2,)),
            dma,
            dma,
        ],
        compiler_params=pltpu.CompilerParams(collective_id=0, has_side_effects=True, vmem_limit_bytes=40 << 20),
        name="adjoint",
    )(jnp.transpose(coupling, (2, 3, 0, 1)), face_map.T, source, inv_diag, wall_jac, ffd_weight, cp_ids)


def solution(mesh):
    in_specs = (
        P(None, "sub", None, "blk"),
        P(None, "sub", None, "blk"),
        P("blk", None, None, None),
        P(),
        P(None, None, None, "sub", "blk"),
        P(None, "sub", "blk"),
        P(None, "sub", "blk"),
    )
    out_specs = (P(None, "sub", None, "blk"), P(None, ("blk", "sub")))
    return jax.shard_map(body, mesh=mesh, in_specs=in_specs, out_specs=out_specs, check_vma=False)
```

```python
import functools

import jax
import jax.numpy as jnp
from jax import lax
from jax.experimental import pallas as pl
from jax.experimental.pallas import tpu as pltpu
from jax.sharding import PartitionSpec as P

MESH = pl.DeviceIdType.MESH
NVAR = 5
CS = 8
CK = 64
CI = 256
SWEEPS = 3
NBLK = 32
NSUB = 4
KT = CK // 8
SPAN_ROWS = ((0, 8), (8, CK - 8))
HALVES = (slice(0, 128), slice(128, 256))


def face_lane(half, tile, row):
    return half * 64 + tile * 8 + row


def place(lane, value, source_lane, target_lane, into):
    shift = lax.rem(target_lane - source_lane + 128, 128)
    return jnp.where(lane == target_lane, pltpu.roll(value, shift, 1), into)


def relax_row(s, p, q, q_pad, coef, src, invd, packed, first=0, end=KT):
    row = lax.broadcasted_iota(jnp.int32, (8, 128), 0)
    lane = lax.broadcasted_iota(jnp.int32, (8, 128), 1)
    zero = jnp.zeros((8, 128), jnp.float32)
    packed = list(packed)
    if first:
        edge = slice(8 * first - 8, 8 * first)
        below = [[pltpu.roll(p[v, s + 1, edge, h], 1, 0) for h in HALVES] for v in range(NVAR)]
    else:
        below = [[zero, zero] for _ in range(NVAR)]
    here = [[p[v, s + 1, 8 * first : 8 * first + 8, h] for h in HALVES] for v in range(NVAR)]
    here_up = [[pltpu.roll(x, 7, 0) for x in pair] for pair in here]
    for t in range(first, end):
        rows = slice(8 * t, 8 * t + 8)
        if t < KT - 1:
            after = [[p[v, s + 1, 8 * t + 8 : 8 * t + 16, h] for h in HALVES] for v in range(NVAR)]
            after_up = [[pltpu.roll(x, 7, 0) for x in pair] for pair in after]
        else:
            after, after_up = None, [[zero, zero]] * NVAR
        acc = [[src[u, s, rows, h] for h in HALVES] for u in range(NVAR)]
        for v in range(NVAR):
            x = here[v]
            down = [pltpu.roll(a, 1, 0) for a in x]
            right = [pltpu.roll(a, 1, 1) for a in x]
            left = [pltpu.roll(a, 127, 1) for a in x]
            nbs = (
                [p[v, s, rows, h] for h in HALVES],
                [p[v, s + 2, rows, h] for h in HALVES],
                [jnp.where(row == 0, a, b) for a, b in zip(below[v], down)],
                [jnp.where(row == 7, a, b) for a, b in zip(after_up[v], here_up[v])],
                [jnp.where(lane == 0, 0.0, right[0]), jnp.where(lane == 0, right[0], right[1])],
                [jnp.where(lane == 127, left[1], left[0]), jnp.where(lane == 127, 0.0, left[1])],
            )
            below[v] = down
            for d in range(6):
                for u in range(NVAR):
                    factor = coef[d * 25 + u * 5 + v]
                    for h in range(2):
                        acc[u][h] = acc[u][h] + factor * nbs[d][h]
        for u in range(NVAR):
            value = [invd[u, s, rows, HALVES[h]] * acc[u][h] for h in range(2)]
            for h in range(2):
                q[u, s + q_pad, rows, HALVES[h]] = value[h]
            if packed:
                both = place(lane, value[1], 127, face_lane(0, t, s), packed[u])
                packed[u] = place(lane, value[0], 0, face_lane(1, t, s), both)
        here, here_up = after, after_up
    return tuple(packed)


def kernel(coup_hbm, fmap_hbm, src_hbm, invd_hbm, wjac_hbm, weight_hbm, ids_hbm, out, sens, coup, fmap, src, invd, wjac, weight, ids, coef,
           p0, p1, p2, fsend, fbuf0, fbuf1, fbuf2, wall, onehot, spread, acc, dense, pair, mine, landing,
           ld_sem, fs_sem, fr_sem, hs_sem, hr_sem, sw_sem, ds_sem, dr_sem):
    blk = lax.axis_index("blk")
    sub = lax.axis_index("sub")
    side, core = sub // 2, lax.rem(sub, 2)
    chip = blk * 2 + side
    lane1 = lax.broadcasted_iota(jnp.int32, (8, 128), 1)
    fields = (p0, p1, p2)
    fbufs = (fbuf0, fbuf1, fbuf2)

    def same_core(other):
        return (other // 2, lax.rem(other, 2) * 2 + core)

    loads = [
        pltpu.make_async_copy(a, b, ld_sem.at[i])
        for i, (a, b) in enumerate((
            (coup_hbm, coup), (fmap_hbm, fmap), (src_hbm, src), (invd_hbm, invd), (wjac_hbm, wjac), (weight_hbm, weight), (ids_hbm, ids)))
    ]
    for copy in loads:
        copy.start()

    barrier = pltpu.get_barrier_semaphore()

    def greet(d, c):
        pl.semaphore_signal(barrier, inc=1, device_id=same_core(lax.rem(chip + d, 64)), device_id_type=MESH)
        return c

    lax.fori_loop(1, 64, greet, 0)
    for step in (1, 3):
        pl.semaphore_signal(barrier, inc=1, device_id=(blk, lax.rem(sub + step, NSUB)), device_id_type=MESH)

    loads[0].wait()
    loads[1].wait()
    for d in range(6):
        for u in range(NVAR):
            for v in range(NVAR):
                coef[d * 25 + u * 5 + v] = jnp.full((8, 128), coup[u, v, 0, d], jnp.float32)

    @pl.when(sub == 0)
    def _():
        for p in fields:
            p[:, 0] = jnp.zeros((NVAR, CK, CI), jnp.float32)

    @pl.when(sub == NSUB - 1)
    def _():
        for p in fields:
            p[:, CS + 1] = jnp.zeros((NVAR, CK, CI), jnp.float32)

    loads[2].wait()
    loads[3].wait()

    def first_row(s, packed):
        face, diag = list(packed[:NVAR]), list(packed[NVAR:])
        for v in range(NVAR):
            for t in range(KT):
                rows = slice(8 * t, 8 * t + 8)
                inv = invd[v, s, rows, :]
                value = inv * src[v, s, rows, :]
                p0[v, s + 1, rows, :] = value
                face[v] = place(lane1, value[:, 128:], 127, face_lane(0, t, s), face[v])
                face[v] = place(lane1, value[:, :128], 0, face_lane(1, t, s), face[v])
                diag[v] = place(lane1, inv[:, :128], 0, face_lane(0, t, s), diag[v])
                diag[v] = place(lane1, inv[:, 128:], 127, face_lane(1, t, s), diag[v])
        return tuple(face + diag)

    none = jnp.zeros((8, 128), jnp.float32)
    packed = lax.fori_loop(0, CS, first_row, (none,) * (2 * NVAR))
    face, diag = packed[:NVAR], packed[NVAR:]

    pl.semaphore_wait(barrier, 65)

    def up_copy(n, i):
        rows = pl.ds(*SPAN_ROWS[i])
        return pltpu.make_async_remote_copy(
            src_ref=fields[n].at[:, CS, rows], dst_ref=fields[n].at[:, 0, rows],
            send_sem=hs_sem.at[n, 0, i], recv_sem=hr_sem.at[n, 0, i],
            device_id=(blk, lax.rem(sub + 1, NSUB)), device_id_type=MESH)

    def down_copy(n, i):
        rows = pl.ds(*SPAN_ROWS[i])
        return pltpu.make_async_remote_copy(
            src_ref=fields[n].at[:, 1, rows], dst_ref=fields[n].at[:, CS + 1, rows],
            send_sem=hs_sem.at[n, 1, i], recv_sem=hr_sem.at[n, 1, i],
            device_id=(blk, lax.rem(sub + NSUB - 1, NSUB)), device_id_type=MESH)

    def start_spans(n):
        for i in range(2):
            pl.when(sub < NSUB - 1)(lambda: up_copy(n, i).start())
            pl.when(sub > 0)(lambda: down_copy(n, i).start())

    def spans_landed(n, i):
        pl.when(sub > 0)(lambda: up_copy(n, i).wait_recv())
        pl.when(sub < NSUB - 1)(lambda: down_copy(n, i).wait_recv())

    def send_faces(n):
        for v in range(NVAR):
            fsend[n, v] = face[v]
            fbufs[n][blk, v] = face[v]

        def send_face(d, c):
            target = lax.rem(blk + d, NBLK)
            pltpu.make_async_remote_copy(
                src_ref=fsend.at[n], dst_ref=fbufs[n].at[blk], send_sem=fs_sem.at[n], recv_sem=fr_sem.at[n],
                device_id=(target, sub), device_id_type=MESH).start()
            return c

        lax.fori_loop(1, NBLK, send_face, 0, unroll=31)

    def faces_landed(n):
        fbuf = fbufs[n]
        landed = fbuf.at[pl.ds(0, NBLK - 1)]
        pltpu.make_async_copy(landed, landed, fr_sem.at[n]).wait()
        low = fbuf[fmap[0, blk]]
        high = fbuf[fmap[1, blk]]
        from_low = lane1 < 64
        outer = [jnp.where(from_low, low[v], high[v]) for v in range(NVAR)]
        terms = []
        for u in range(NVAR):
            total = none
            for v in range(NVAR):
                total = total + jnp.where(from_low, coef[100 + u * 5 + v], coef[125 + u * 5 + v]) * outer[v]
            terms.append(diag[u] * total)
        return terms

    def add_faces(p, pad, s, terms, tiles=(0, KT)):
        for u in range(NVAR):
            for t in range(*tiles):
                rows = slice(8 * t, 8 * t + 8)
                low = place(lane1, terms[u], face_lane(0, t, s), 0, 0.0)
                high = place(lane1, terms[u], face_lane(1, t, s), 127, 0.0)
                p[u, s + pad, rows, 0:128] = p[u, s + pad, rows, 0:128] + low
                p[u, s + pad, rows, 128:256] = p[u, s + pad, rows, 128:256] + high

    def over(rows, step):
        lo, hi = rows
        lax.fori_loop(lo, hi, lambda s, c: (step(s), c)[1], 0)

    def ends(step):
        lax.fori_loop(0, 2, lambda i, c: (step(i * (CS - 1)), c)[1], 0)

    for n in range(SWEEPS - 1):
        p, q = fields[n], fields[n + 1]
        send_faces(n)
        if n > 0:
            ends(lambda s: add_faces(p, 1, s, extra))
        start_spans(n)
        if n > 0:
            over((1, CS - 1), lambda s: add_faces(p, 1, s, extra))
        step = lambda s, c: relax_row(s, p, q, 1, coef, src, invd, c)
        made = lax.fori_loop(1, CS - 1, step, (none,) * NVAR)
        spans_landed(n, 0)
        spans_landed(n, 1)
        made = lax.fori_loop(0, 2, lambda i, c: step(i * (CS - 1), c), made)
        extra = faces_landed(n)
        face = [made[u] + pltpu.roll(extra[u], 64, 1) for u in range(NVAR)]

    n = SWEEPS - 1
    p = fields[n]
    send_faces(n)
    ends(lambda s: add_faces(p, 1, s, extra))
    start_spans(n)
    over((1, CS - 1), lambda s: add_faces(p, 1, s, extra))

    def last_rows(s, first, end):
        relax_row(s, p, out, 0, coef, src, invd, (), first, end)

    over((1, CS - 1), lambda s: last_rows(s, 0, 1))
    over((1, 3), lambda s: last_rows(s, 1, KT))
    spans_landed(n, 0)
    ends(lambda s: last_rows(s, 0, 1))
    for copy in loads[4:]:
        copy.wait()

    def wall_of(c):
        total = jnp.zeros((CS, CI), jnp.float32)
        for v in range(NVAR):
            for k in range(2):
                total = total + wjac[c, v, k] * out[v, :, k, :]
        return total

    column = lax.broadcasted_iota(jnp.int32, (CS, CI), 1)
    inner = (column > 0) & (column < CI - 1)
    for c in range(3):
        wall[c] = jnp.where(inner, wall_of(c), 0.0)

    acc[...] = jnp.zeros_like(acc)

    def row_and_lane(point):
        high = point >> 7
        holder = (high * 171) >> 9
        order = (holder & 1) * 64 + (holder >> 1)
        return jnp.where(point < 0, -1, (high - 3 * holder) * 128 + order), point & 127

    def slots(m, carry):
        rank, low = row_and_lane(ids[m])
        pieces = []
        for c in range(3):
            value = weight[m] * wall[c]
            top = value.astype(jnp.bfloat16).astype(jnp.float32)
            pieces.append(top)
            pieces.append(value - top)
        for s in range(CS):
            lanes = slice(s * CI, (s + 1) * CI)
            hit = lax.broadcasted_iota(jnp.int32, (384, CI), 0) == rank[s : s + 1, :]
            onehot[:, lanes] = jnp.where(hit, 1.0, 0.0).astype(jnp.bfloat16)
            match = lax.broadcasted_iota(jnp.int32, (128, CI), 0) == low[s : s + 1, :]
            for i in range(6):
                spread[i * 128 : (i + 1) * 128, lanes] = jnp.where(match, pieces[i][s : s + 1, :], 0.0).astype(jnp.bfloat16)
        acc[...] = acc[...] + lax.dot_general(
            onehot[...], spread[...], (((1,), (1,)), ((), ())), preferred_element_type=jnp.float32)
        return carry

    lax.fori_loop(0, 8, slots, 0)

    extra = faces_landed(n)
    over((0, CS), lambda s: add_faces(out, 0, s, extra, (0, 1)))
    walls = [wall_of(c) for c in range(3)]
    marks = [jnp.full((8, 128), -1, jnp.int32), jnp.zeros((8, 128), jnp.int32)] + [none] * 3
    for m in range(8):
        rank, low = row_and_lane(ids[m])
        for i, x in enumerate([rank, low] + [weight[m] * walls[c] for c in range(3)]):
            marks[i] = place(lane1, x[:, :128], 0, 2 * m, marks[i])
            marks[i] = place(lane1, x[:, 128:], 127, 2 * m + 1, marks[i])
    line = lax.broadcasted_iota(jnp.int32, (1, 128), 1)
    flat = []
    for x in marks:
        total = x[0:1, :]
        for s in range(1, CS):
            total = jnp.where((line >> 4) == s, pltpu.roll(x[s : s + 1, :], 16 * s, 1), total)
        flat.append(total)
    hit = lax.broadcasted_iota(jnp.int32, (384, 128), 0) == flat[0]
    match = lax.broadcasted_iota(jnp.int32, (128, 128), 0) == flat[1]
    edge_spread = []
    for c in range(3):
        top = flat[2 + c].astype(jnp.bfloat16).astype(jnp.float32)
        for value in (top, flat[2 + c] - top):
            edge_spread.append(jnp.where(match, value, 0.0).astype(jnp.bfloat16))
    acc[...] = acc[...] + lax.dot_general(
        jnp.where(hit, 1.0, 0.0).astype(jnp.bfloat16), jnp.concatenate(edge_spread, 0), (((1,), (1,)), ((), ())),
        preferred_element_type=jnp.float32)
    for j in range(3):
        for c in range(3):
            for g in range(16):
                rows = slice(j * 128 + g * 8, j * 128 + g * 8 + 8)
                total = acc[rows, c * 256 : c * 256 + 128] + acc[rows, c * 256 + 128 : c * 256 + 256]
                dense[pl.ds(g * 128 + c * 3 + j, 8, stride=16), :] = total

    swap = pltpu.make_async_remote_copy(
        src_ref=dense.at[pl.ds((1 - core) * 1024, 1024)], dst_ref=pair, send_sem=sw_sem.at[0], recv_sem=sw_sem.at[1],
        device_id=(blk, side * 2 + 1 - core), device_id_type=MESH)
    swap.start()
    swap.wait()

    def add(i, c):
        both = dense[pl.ds(core * 1024 + i * 16, 16), :] + pair[pl.ds(i * 16, 16), :]
        mine[i] = both[:9, :]
        return c

    lax.fori_loop(0, 64, add, 0, unroll=8)

    def send_points(d, c):
        other = lax.rem(chip + d, 64)
        pltpu.make_async_remote_copy(
            src_ref=mine.at[other], dst_ref=landing.at[d], send_sem=ds_sem, recv_sem=dr_sem,
            device_id=same_core(other), device_id_type=MESH).start()
        return c

    lax.fori_loop(1, 64, send_points, 0, unroll=9)
    landing[0] = mine[chip]

    spans_landed(n, 1)
    over((3, CS - 1), lambda s: last_rows(s, 1, KT))
    ends(lambda s: last_rows(s, 1, KT))
    over((0, CS), lambda s: add_faces(out, 0, s, extra, (1, KT)))

    landed = landing.at[pl.ds(1, 63)]
    pltpu.make_async_copy(landed, landed, dr_sem).wait()
    total = lax.fori_loop(0, 64, lambda i, t: t + landing[i], jnp.zeros((9, 128), jnp.float32), unroll=8)
    for c in range(3):
        for j in range(3):
            sens[c : c + 1, j * 128 : (j + 1) * 128] = total[c * 3 + j : c * 3 + j + 1, :]
    pltpu.make_async_copy(landed, landed, ds_sem).wait()

    for n in range(SWEEPS):
        for i in range(2):
            pl.when(sub < NSUB - 1)(lambda: up_copy(n, i).wait_send())
            pl.when(sub > 0)(lambda: down_copy(n, i).wait_send())
        sent = fbufs[n].at[pl.ds(0, NBLK - 1)]
        pltpu.make_async_copy(sent, sent, fs_sem.at[n]).wait()


def body(source, inv_diag, coupling, face_map, wall_jac, ffd_weight, cp_ids):
    vmem = pl.BlockSpec(memory_space=pltpu.VMEM)
    hbm = pl.BlockSpec(memory_space=pltpu.HBM)
    f32, dma = jnp.float32, pltpu.SemaphoreType.DMA
    args = (jnp.transpose(coupling, (2, 3, 0, 1)), face_map.T, source, inv_diag, wall_jac, ffd_weight, cp_ids)
    face_buffer = pltpu.VMEM((NBLK, NVAR, 8, 128), f32)
    field = pltpu.VMEM((NVAR, CS + 2, CK, CI), f32)
    return pl.pallas_call(
        kernel,
        out_shape=(jax.ShapeDtypeStruct((NVAR, CS, CK, CI), f32), jax.ShapeDtypeStruct((3, 384), f32)),
        in_specs=[hbm] * 7,
        out_specs=(vmem, vmem),
        scratch_shapes=[
            pltpu.SMEM((NVAR, NVAR, 1, 6), f32),
            pltpu.SMEM((2, NBLK), jnp.int32),
            pltpu.VMEM((NVAR, CS, CK, CI), f32),
            pltpu.VMEM((NVAR, CS, CK, CI), f32),
            pltpu.VMEM((3, NVAR, 2, CS, CI), f32),
            pltpu.VMEM((8, CS, CI), f32),
            pltpu.VMEM((8, CS, CI), jnp.int32),
            pltpu.VMEM((150, 8, 128), f32),
            field,
            field,
            field,
            pltpu.VMEM((SWEEPS, NVAR, 8, 128), f32),
            face_buffer,
            face_buffer,
            face_buffer,
            pltpu.VMEM((3, CS, CI), f32),
            pltpu.VMEM((384, CS * CI), jnp.bfloat16),
            pltpu.VMEM((768, CS * CI), jnp.bfloat16),
            pltpu.VMEM((384, 768), f32),
            pltpu.VMEM((2048, 128), f32),
            pltpu.VMEM((1024, 128), f32),
            pltpu.VMEM((64, 9, 128), f32),
            pltpu.VMEM((64, 9, 128), f32),
            dma((7,)),
            dma((SWEEPS,)),
            dma((SWEEPS,)),
            dma((SWEEPS, 2, 2)),
            dma((SWEEPS, 2, 2)),
            dma((2,)),
            dma,
            dma,
        ],
        compiler_params=pltpu.CompilerParams(collective_id=0, has_side_effects=True, vmem_limit_bytes=40 << 20),
        name="adjoint",
    )(*[pltpu.with_memory_space_constraint(x, pltpu.HBM) for x in args])


def solution(mesh):
    in_specs = (
        P(None, "sub", None, "blk"),
        P(None, "sub", None, "blk"),
        P("blk", None, None, None),
        P(),
        P(None, None, None, "sub", "blk"),
        P(None, "sub", "blk"),
        P(None, "sub", "blk"),
    )
    out_specs = (P(None, "sub", None, "blk"), P(None, ("blk", "sub")))
    return jax.shard_map(body, mesh=mesh, in_specs=in_specs, out_specs=out_specs, check_vma=False)
```

```python
import functools

import jax
import jax.numpy as jnp
from jax import lax
from jax.experimental import pallas as pl
from jax.experimental.pallas import tpu as pltpu
from jax.sharding import PartitionSpec as P

MESH = pl.DeviceIdType.MESH
NVAR = 5
CS = 8
CK = 64
CI = 256
SWEEPS = 3
NBLK = 32
NSUB = 4
KT = CK // 8
SPAN_ROWS = ((0, 8), (8, CK - 8))
HALVES = (slice(0, 128), slice(128, 256))


def hops(offset):
    dh, dx, dz, dl = offset
    return (0, 1, 2, 1)[dx] + (0, 1, 2, 1)[dz] + (2 * (1 - dl) if dh else dl) + (dh * dl)


CHIPS = [(dh, dx, dz, dl) for dh in range(2) for dx in range(4) for dz in range(4) for dl in range(2)]
FAR_CHIPS = sorted(CHIPS[1:], key=lambda offset: -hops(offset))
FAR_BLOCKS = [offset for offset in FAR_CHIPS if not offset[3]]


def face_lane(half, tile, row):
    return half * 64 + tile * 8 + row


def place(lane, value, source_lane, target_lane, into):
    shift = lax.rem(target_lane - source_lane + 128, 128)
    return jnp.where(lane == target_lane, pltpu.roll(value, shift, 1), into)


def relax_row(s, p, q, q_pad, coef, src, invd, packed, first=0, end=KT):
    row = lax.broadcasted_iota(jnp.int32, (8, 128), 0)
    lane = lax.broadcasted_iota(jnp.int32, (8, 128), 1)
    zero = jnp.zeros((8, 128), jnp.float32)
    packed = list(packed)
    if first:
        edge = slice(8 * first - 8, 8 * first)
        below = [[pltpu.roll(p[v, s + 1, edge, h], 1, 0) for h in HALVES] for v in range(NVAR)]
    else:
        below = [[zero, zero] for _ in range(NVAR)]
    here = [[p[v, s + 1, 8 * first : 8 * first + 8, h] for h in HALVES] for v in range(NVAR)]
    here_up = [[pltpu.roll(x, 7, 0) for x in pair] for pair in here]
    for t in range(first, end):
        rows = slice(8 * t, 8 * t + 8)
        if t < KT - 1:
            after = [[p[v, s + 1, 8 * t + 8 : 8 * t + 16, h] for h in HALVES] for v in range(NVAR)]
            after_up = [[pltpu.roll(x, 7, 0) for x in pair] for pair in after]
        else:
            after, after_up = None, [[zero, zero]] * NVAR
        acc = [[src[u, s, rows, h] for h in HALVES] for u in range(NVAR)]
        for v in range(NVAR):
            x = here[v]
            down = [pltpu.roll(a, 1, 0) for a in x]
            right = [pltpu.roll(a, 1, 1) for a in x]
            left = [pltpu.roll(a, 127, 1) for a in x]
            nbs = (
                [p[v, s, rows, h] for h in HALVES],
                [p[v, s + 2, rows, h] for h in HALVES],
                [jnp.where(row == 0, a, b) for a, b in zip(below[v], down)],
                [jnp.where(row == 7, a, b) for a, b in zip(after_up[v], here_up[v])],
                [jnp.where(lane == 0, 0.0, right[0]), jnp.where(lane == 0, right[0], right[1])],
                [jnp.where(lane == 127, left[1], left[0]), jnp.where(lane == 127, 0.0, left[1])],
            )
            below[v] = down
            for d in range(6):
                for u in range(NVAR):
                    factor = coef[d * 25 + u * 5 + v]
                    for h in range(2):
                        acc[u][h] = acc[u][h] + factor * nbs[d][h]
        for u in range(NVAR):
            value = [invd[u, s, rows, HALVES[h]] * acc[u][h] for h in range(2)]
            for h in range(2):
                q[u, s + q_pad, rows, HALVES[h]] = value[h]
            if packed:
                both = place(lane, value[1], 127, face_lane(0, t, s), packed[u])
                packed[u] = place(lane, value[0], 0, face_lane(1, t, s), both)
        here, here_up = after, after_up
    return tuple(packed)


def kernel(coup_hbm, fmap_hbm, src_hbm, invd_hbm, wjac_hbm, weight_hbm, ids_hbm, out, sens, coup, fmap, src, invd, wjac, weight, ids, coef,
           p0, p1, p2, fsend, fbuf0, fbuf1, fbuf2, wall, onehot, spread, acc, dense, pair, mine, landing,
           ld_sem, fs_sem, fr_sem, hs_sem, hr_sem, sw_sem, ds_sem, dr_sem):
    blk = lax.axis_index("blk")
    sub = lax.axis_index("sub")
    side, core = sub // 2, lax.rem(sub, 2)
    chip = blk * 2 + side
    lane1 = lax.broadcasted_iota(jnp.int32, (8, 128), 1)
    fields = (p0, p1, p2)
    fbufs = (fbuf0, fbuf1, fbuf2)

    high_y, at_x, at_z = lax.div(blk, 16), lax.rem(lax.div(blk, 4), 4), lax.rem(blk, 4)

    def moved(offset):
        dh, dx, dz, dl = offset
        other = lax.rem(high_y + dh, 2) * 16 + lax.rem(at_x + dx, 4) * 4 + lax.rem(at_z + dz, 4)
        return other, lax.rem(side + dl, 2)

    def same_core(offset):
        other, other_side = moved(offset)
        return (other, other_side * 2 + core)

    loads = [
        pltpu.make_async_copy(a, b, ld_sem.at[i])
        for i, (a, b) in enumerate((
            (coup_hbm, coup), (fmap_hbm, fmap), (src_hbm, src), (invd_hbm, invd), (wjac_hbm, wjac), (weight_hbm, weight), (ids_hbm, ids)))
    ]
    for copy in loads:
        copy.start()

    barrier = pltpu.get_barrier_semaphore()

    for offset in FAR_CHIPS:
        pl.semaphore_signal(barrier, inc=1, device_id=same_core(offset), device_id_type=MESH)
    for step in (1, 3):
        pl.semaphore_signal(barrier, inc=1, device_id=(blk, lax.rem(sub + step, NSUB)), device_id_type=MESH)

    loads[0].wait()
    loads[1].wait()
    for d in range(6):
        for u in range(NVAR):
            for v in range(NVAR):
                coef[d * 25 + u * 5 + v] = jnp.full((8, 128), coup[u, v, 0, d], jnp.float32)

    @pl.when(sub == 0)
    def _():
        for p in fields:
            p[:, 0] = jnp.zeros((NVAR, CK, CI), jnp.float32)

    @pl.when(sub == NSUB - 1)
    def _():
        for p in fields:
            p[:, CS + 1] = jnp.zeros((NVAR, CK, CI), jnp.float32)

    loads[2].wait()
    loads[3].wait()

    def first_row(s, packed):
        face, diag = list(packed[:NVAR]), list(packed[NVAR:])
        for v in range(NVAR):
            for t in range(KT):
                rows = slice(8 * t, 8 * t + 8)
                inv = invd[v, s, rows, :]
                value = inv * src[v, s, rows, :]
                p0[v, s + 1, rows, :] = value
                face[v] = place(lane1, value[:, 128:], 127, face_lane(0, t, s), face[v])
                face[v] = place(lane1, value[:, :128], 0, face_lane(1, t, s), face[v])
                diag[v] = place(lane1, inv[:, :128], 0, face_lane(0, t, s), diag[v])
                diag[v] = place(lane1, inv[:, 128:], 127, face_lane(1, t, s), diag[v])
        return tuple(face + diag)

    none = jnp.zeros((8, 128), jnp.float32)
    packed = lax.fori_loop(0, CS, first_row, (none,) * (2 * NVAR))
    face, diag = packed[:NVAR], packed[NVAR:]

    pl.semaphore_wait(barrier, 65)

    def up_copy(n, i):
        rows = pl.ds(*SPAN_ROWS[i])
        return pltpu.make_async_remote_copy(
            src_ref=fields[n].at[:, CS, rows], dst_ref=fields[n].at[:, 0, rows],
            send_sem=hs_sem.at[n, 0, i], recv_sem=hr_sem.at[n, 0, i],
            device_id=(blk, lax.rem(sub + 1, NSUB)), device_id_type=MESH)

    def down_copy(n, i):
        rows = pl.ds(*SPAN_ROWS[i])
        return pltpu.make_async_remote_copy(
            src_ref=fields[n].at[:, 1, rows], dst_ref=fields[n].at[:, CS + 1, rows],
            send_sem=hs_sem.at[n, 1, i], recv_sem=hr_sem.at[n, 1, i],
            device_id=(blk, lax.rem(sub + NSUB - 1, NSUB)), device_id_type=MESH)

    def start_spans(n):
        for i in range(2):
            pl.when(sub < NSUB - 1)(lambda: up_copy(n, i).start())
            pl.when(sub > 0)(lambda: down_copy(n, i).start())

    def spans_landed(n, i):
        pl.when(sub > 0)(lambda: up_copy(n, i).wait_recv())
        pl.when(sub < NSUB - 1)(lambda: down_copy(n, i).wait_recv())

    def send_faces(n):
        for v in range(NVAR):
            fsend[n, v] = face[v]
            fbufs[n][blk, v] = face[v]

        for offset in FAR_BLOCKS:
            pltpu.make_async_remote_copy(
                src_ref=fsend.at[n], dst_ref=fbufs[n].at[blk], send_sem=fs_sem.at[n], recv_sem=fr_sem.at[n],
                device_id=same_core(offset), device_id_type=MESH).start()

    def faces_landed(n):
        fbuf = fbufs[n]
        landed = fbuf.at[pl.ds(0, NBLK - 1)]
        pltpu.make_async_copy(landed, landed, fr_sem.at[n]).wait()
        low = fbuf[fmap[0, blk]]
        high = fbuf[fmap[1, blk]]
        from_low = lane1 < 64
        outer = [jnp.where(from_low, low[v], high[v]) for v in range(NVAR)]
        terms = []
        for u in range(NVAR):
            total = none
            for v in range(NVAR):
                total = total + jnp.where(from_low, coef[100 + u * 5 + v], coef[125 + u * 5 + v]) * outer[v]
            terms.append(diag[u] * total)
        return terms

    def add_faces(p, pad, s, terms, tiles=(0, KT)):
        for u in range(NVAR):
            for t in range(*tiles):
                rows = slice(8 * t, 8 * t + 8)
                low = place(lane1, terms[u], face_lane(0, t, s), 0, 0.0)
                high = place(lane1, terms[u], face_lane(1, t, s), 127, 0.0)
                p[u, s + pad, rows, 0:128] = p[u, s + pad, rows, 0:128] + low
                p[u, s + pad, rows, 128:256] = p[u, s + pad, rows, 128:256] + high

    def over(rows, step):
        lo, hi = rows
        lax.fori_loop(lo, hi, lambda s, c: (step(s), c)[1], 0)

    def ends(step):
        lax.fori_loop(0, 2, lambda i, c: (step(i * (CS - 1)), c)[1], 0)

    for n in range(SWEEPS - 1):
        p, q = fields[n], fields[n + 1]
        send_faces(n)
        if n > 0:
            ends(lambda s: add_faces(p, 1, s, extra))
        start_spans(n)
        if n > 0:
            over((1, CS - 1), lambda s: add_faces(p, 1, s, extra))
        step = lambda s, c: relax_row(s, p, q, 1, coef, src, invd, c)
        made = lax.fori_loop(1, CS - 1, step, (none,) * NVAR)
        spans_landed(n, 0)
        spans_landed(n, 1)
        made = lax.fori_loop(0, 2, lambda i, c: step(i * (CS - 1), c), made)
        extra = faces_landed(n)
        face = [made[u] + pltpu.roll(extra[u], 64, 1) for u in range(NVAR)]

    n = SWEEPS - 1
    p = fields[n]
    send_faces(n)
    ends(lambda s: add_faces(p, 1, s, extra))
    start_spans(n)
    over((1, CS - 1), lambda s: add_faces(p, 1, s, extra))

    def last_rows(s, first, end):
        relax_row(s, p, out, 0, coef, src, invd, (), first, end)

    over((1, CS - 1), lambda s: last_rows(s, 0, 1))
    over((1, 3), lambda s: last_rows(s, 1, KT))
    spans_landed(n, 0)
    ends(lambda s: last_rows(s, 0, 1))
    for copy in loads[4:]:
        copy.wait()

    def wall_of(c):
        total = jnp.zeros((CS, CI), jnp.float32)
        for v in range(NVAR):
            for k in range(2):
                total = total + wjac[c, v, k] * out[v, :, k, :]
        return total

    column = lax.broadcasted_iota(jnp.int32, (CS, CI), 1)
    inner = (column > 0) & (column < CI - 1)
    for c in range(3):
        wall[c] = jnp.where(inner, wall_of(c), 0.0)

    acc[...] = jnp.zeros_like(acc)

    def row_and_lane(point):
        high = point >> 7
        holder = (high * 171) >> 9
        order = (holder & 1) * 64 + (holder >> 1)
        return jnp.where(point < 0, -1, (high - 3 * holder) * 128 + order), point & 127

    def slots(step, carry):
        for i in range(2):
            m = 2 * step + i
            rank, low = row_and_lane(ids[m])
            pieces = []
            for c in range(3):
                value = weight[m] * wall[c]
                top = value.astype(jnp.bfloat16).astype(jnp.float32)
                pieces.append(top)
                pieces.append(value - top)
            for s in range(CS):
                lanes = slice((i * CS + s) * CI, (i * CS + s + 1) * CI)
                hit = lax.broadcasted_iota(jnp.int32, (384, CI), 0) == rank[s : s + 1, :]
                onehot[:, lanes] = jnp.where(hit, 1.0, 0.0).astype(jnp.bfloat16)
                match = lax.broadcasted_iota(jnp.int32, (128, CI), 0) == low[s : s + 1, :]
                for k in range(6):
                    spread[k * 128 : (k + 1) * 128, lanes] = jnp.where(match, pieces[k][s : s + 1, :], 0.0).astype(jnp.bfloat16)
        acc[...] = acc[...] + lax.dot_general(
            onehot[...], spread[...], (((1,), (1,)), ((), ())), preferred_element_type=jnp.float32)
        return carry

    lax.fori_loop(0, 4, slots, 0)

    extra = faces_landed(n)
    over((0, CS), lambda s: add_faces(out, 0, s, extra, (0, 1)))
    walls = [wall_of(c) for c in range(3)]
    marks = [jnp.full((8, 128), -1, jnp.int32), jnp.zeros((8, 128), jnp.int32)] + [none] * 3
    for m in range(8):
        rank, low = row_and_lane(ids[m])
        for i, x in enumerate([rank, low] + [weight[m] * walls[c] for c in range(3)]):
            marks[i] = place(lane1, x[:, :128], 0, 2 * m, marks[i])
            marks[i] = place(lane1, x[:, 128:], 127, 2 * m + 1, marks[i])
    line = lax.broadcasted_iota(jnp.int32, (1, 128), 1)
    flat = []
    for x in marks:
        total = x[0:1, :]
        for s in range(1, CS):
            total = jnp.where((line >> 4) == s, pltpu.roll(x[s : s + 1, :], 16 * s, 1), total)
        flat.append(total)
    hit = lax.broadcasted_iota(jnp.int32, (384, 128), 0) == flat[0]
    match = lax.broadcasted_iota(jnp.int32, (128, 128), 0) == flat[1]
    edge_spread = []
    for c in range(3):
        top = flat[2 + c].astype(jnp.bfloat16).astype(jnp.float32)
        for value in (top, flat[2 + c] - top):
            edge_spread.append(jnp.where(match, value, 0.0).astype(jnp.bfloat16))
    acc[...] = acc[...] + lax.dot_general(
        jnp.where(hit, 1.0, 0.0).astype(jnp.bfloat16), jnp.concatenate(edge_spread, 0), (((1,), (1,)), ((), ())),
        preferred_element_type=jnp.float32)
    for j in range(3):
        for c in range(3):
            for g in range(16):
                rows = slice(j * 128 + g * 8, j * 128 + g * 8 + 8)
                total = acc[rows, c * 256 : c * 256 + 128] + acc[rows, c * 256 + 128 : c * 256 + 256]
                dense[pl.ds(g * 128 + c * 3 + j, 8, stride=16), :] = total

    swap = pltpu.make_async_remote_copy(
        src_ref=dense.at[pl.ds((1 - core) * 1024, 1024)], dst_ref=pair, send_sem=sw_sem.at[0], recv_sem=sw_sem.at[1],
        device_id=(blk, side * 2 + 1 - core), device_id_type=MESH)
    swap.start()
    swap.wait()

    def add(i, c):
        both = dense[pl.ds(core * 1024 + i * 16, 16), :] + pair[pl.ds(i * 16, 16), :]
        mine[i] = both[:9, :]
        return c

    lax.fori_loop(0, 64, add, 0, unroll=8)

    for d, offset in enumerate(FAR_CHIPS):
        other, other_side = moved(offset)
        pltpu.make_async_remote_copy(
            src_ref=mine.at[other * 2 + other_side], dst_ref=landing.at[d + 1], send_sem=ds_sem, recv_sem=dr_sem,
            device_id=same_core(offset), device_id_type=MESH).start()
    landing[0] = mine[chip]

    spans_landed(n, 1)
    over((3, CS - 1), lambda s: last_rows(s, 1, KT))
    ends(lambda s: last_rows(s, 1, KT))
    over((0, CS), lambda s: add_faces(out, 0, s, extra, (1, KT)))

    landed = landing.at[pl.ds(1, 63)]
    pltpu.make_async_copy(landed, landed, dr_sem).wait()
    total = lax.fori_loop(0, 64, lambda i, t: t + landing[i], jnp.zeros((9, 128), jnp.float32), unroll=8)
    for c in range(3):
        for j in range(3):
            sens[c : c + 1, j * 128 : (j + 1) * 128] = total[c * 3 + j : c * 3 + j + 1, :]
    pltpu.make_async_copy(landed, landed, ds_sem).wait()

    for n in range(SWEEPS):
        for i in range(2):
            pl.when(sub < NSUB - 1)(lambda: up_copy(n, i).wait_send())
            pl.when(sub > 0)(lambda: down_copy(n, i).wait_send())
        sent = fbufs[n].at[pl.ds(0, NBLK - 1)]
        pltpu.make_async_copy(sent, sent, fs_sem.at[n]).wait()


def body(source, inv_diag, coupling, face_map, wall_jac, ffd_weight, cp_ids):
    vmem = pl.BlockSpec(memory_space=pltpu.VMEM)
    hbm = pl.BlockSpec(memory_space=pltpu.HBM)
    f32, dma = jnp.float32, pltpu.SemaphoreType.DMA
    args = (jnp.transpose(coupling, (2, 3, 0, 1)), face_map.T, source, inv_diag, wall_jac, ffd_weight, cp_ids)
    face_buffer = pltpu.VMEM((NBLK, NVAR, 8, 128), f32)
    field = pltpu.VMEM((NVAR, CS + 2, CK, CI), f32)
    return pl.pallas_call(
        kernel,
        out_shape=(jax.ShapeDtypeStruct((NVAR, CS, CK, CI), f32), jax.ShapeDtypeStruct((3, 384), f32)),
        in_specs=[hbm] * 7,
        out_specs=(vmem, vmem),
        scratch_shapes=[
            pltpu.SMEM((NVAR, NVAR, 1, 6), f32),
            pltpu.SMEM((2, NBLK), jnp.int32),
            pltpu.VMEM((NVAR, CS, CK, CI), f32),
            pltpu.VMEM((NVAR, CS, CK, CI), f32),
            pltpu.VMEM((3, NVAR, 2, CS, CI), f32),
            pltpu.VMEM((8, CS, CI), f32),
            pltpu.VMEM((8, CS, CI), jnp.int32),
            pltpu.VMEM((150, 8, 128), f32),
            field,
            field,
            field,
            pltpu.VMEM((SWEEPS, NVAR, 8, 128), f32),
            face_buffer,
            face_buffer,
            face_buffer,
            pltpu.VMEM((3, CS, CI), f32),
            pltpu.VMEM((384, 2 * CS * CI), jnp.bfloat16),
            pltpu.VMEM((768, 2 * CS * CI), jnp.bfloat16),
            pltpu.VMEM((384, 768), f32),
            pltpu.VMEM((2048, 128), f32),
            pltpu.VMEM((1024, 128), f32),
            pltpu.VMEM((64, 9, 128), f32),
            pltpu.VMEM((64, 9, 128), f32),
            dma((7,)),
            dma((SWEEPS,)),
            dma((SWEEPS,)),
            dma((SWEEPS, 2, 2)),
            dma((SWEEPS, 2, 2)),
            dma((2,)),
            dma,
            dma,
        ],
        compiler_params=pltpu.CompilerParams(collective_id=0, has_side_effects=True, vmem_limit_bytes=44 << 20),
        name="adjoint",
    )(*[pltpu.with_memory_space_constraint(x, pltpu.HBM) for x in args])


def solution(mesh):
    in_specs = (
        P(None, "sub", None, "blk"),
        P(None, "sub", None, "blk"),
        P("blk", None, None, None),
        P(),
        P(None, None, None, "sub", "blk"),
        P(None, "sub", "blk"),
        P(None, "sub", "blk"),
    )
    out_specs = (P(None, "sub", None, "blk"), P(None, ("blk", "sub")))
    return jax.shard_map(body, mesh=mesh, in_specs=in_specs, out_specs=out_specs, check_vma=False)
```

```python
import functools

import jax
import jax.numpy as jnp
from jax import lax
from jax.experimental import pallas as pl
from jax.experimental.pallas import tpu as pltpu
from jax.sharding import PartitionSpec as P

MESH = pl.DeviceIdType.MESH
NVAR = 5
CS = 8
CK = 64
CI = 256
SWEEPS = 3
NBLK = 32
NSUB = 4
KT = CK // 8
SPAN_ROWS = ((0, 8), (8, CK - 8))
HALVES = (slice(0, 128), slice(128, 256))


def hops(offset):
    dh, dx, dz, dl = offset
    return (0, 1, 2, 1)[dx] + (0, 1, 2, 1)[dz] + (2 * (1 - dl) if dh else dl) + (dh * dl)


CHIPS = [(dh, dx, dz, dl) for dh in range(2) for dx in range(4) for dz in range(4) for dl in range(2)]
FAR_CHIPS = sorted(CHIPS[1:], key=lambda offset: -hops(offset))
FAR_BLOCKS = [offset for offset in FAR_CHIPS if not offset[3]]


def face_lane(half, tile, row):
    return half * 64 + tile * 8 + row


def place(lane, value, source_lane, target_lane, into):
    shift = lax.rem(target_lane - source_lane + 128, 128)
    return jnp.where(lane == target_lane, pltpu.roll(value, shift, 1), into)


def relax_row(s, p, q, q_pad, coef, src, invd, packed, first=0, end=KT):
    row = lax.broadcasted_iota(jnp.int32, (8, 128), 0)
    lane = lax.broadcasted_iota(jnp.int32, (8, 128), 1)
    zero = jnp.zeros((8, 128), jnp.float32)
    packed = list(packed)
    if first:
        edge = slice(8 * first - 8, 8 * first)
        below = [[pltpu.roll(p[v, s + 1, edge, h], 1, 0) for h in HALVES] for v in range(NVAR)]
    else:
        below = [[zero, zero] for _ in range(NVAR)]
    here = [[p[v, s + 1, 8 * first : 8 * first + 8, h] for h in HALVES] for v in range(NVAR)]
    here_up = [[pltpu.roll(x, 7, 0) for x in pair] for pair in here]
    for t in range(first, end):
        rows = slice(8 * t, 8 * t + 8)
        if t < KT - 1:
            after = [[p[v, s + 1, 8 * t + 8 : 8 * t + 16, h] for h in HALVES] for v in range(NVAR)]
            after_up = [[pltpu.roll(x, 7, 0) for x in pair] for pair in after]
        else:
            after, after_up = None, [[zero, zero]] * NVAR
        acc = [[src[u, s, rows, h] for h in HALVES] for u in range(NVAR)]
        for v in range(NVAR):
            x = here[v]
            down = [pltpu.roll(a, 1, 0) for a in x]
            right = [pltpu.roll(a, 1, 1) for a in x]
            left = [pltpu.roll(a, 127, 1) for a in x]
            nbs = (
                [p[v, s, rows, h] for h in HALVES],
                [p[v, s + 2, rows, h] for h in HALVES],
                [jnp.where(row == 0, a, b) for a, b in zip(below[v], down)],
                [jnp.where(row == 7, a, b) for a, b in zip(after_up[v], here_up[v])],
                [jnp.where(lane == 0, 0.0, right[0]), jnp.where(lane == 0, right[0], right[1])],
                [jnp.where(lane == 127, left[1], left[0]), jnp.where(lane == 127, 0.0, left[1])],
            )
            below[v] = down
            for d in range(6):
                for u in range(NVAR):
                    factor = coef[d * 25 + u * 5 + v]
                    for h in range(2):
                        acc[u][h] = acc[u][h] + factor * nbs[d][h]
        for u in range(NVAR):
            value = [invd[u, s, rows, HALVES[h]] * acc[u][h] for h in range(2)]
            for h in range(2):
                q[u, s + q_pad, rows, HALVES[h]] = value[h]
            if packed:
                both = place(lane, value[1], 127, face_lane(0, t, s), packed[u])
                packed[u] = place(lane, value[0], 0, face_lane(1, t, s), both)
        here, here_up = after, after_up
    return tuple(packed)


def kernel(coup_hbm, fmap_hbm, src_hbm, invd_hbm, wjac_hbm, weight_hbm, ids_hbm, out, sens, coup, fmap, src, invd, wjac, weight, ids, coef,
           p0, p1, p2, fsend, fbuf0, fbuf1, fbuf2, wall, onehot, spread, acc, dense, pair, mine, landing,
           ld_sem, fs_sem, fr_sem, hs_sem, hr_sem, sw_sem, ds_sem, dr_sem):
    blk = lax.axis_index("blk")
    sub = lax.axis_index("sub")
    side, core = sub // 2, lax.rem(sub, 2)
    chip = blk * 2 + side
    lane1 = lax.broadcasted_iota(jnp.int32, (8, 128), 1)
    fields = (p0, p1, p2)
    fbufs = (fbuf0, fbuf1, fbuf2)

    high_y, at_x, at_z = lax.div(blk, 16), lax.rem(lax.div(blk, 4), 4), lax.rem(blk, 4)

    def moved(offset):
        dh, dx, dz, dl = offset
        other = lax.rem(high_y + dh, 2) * 16 + lax.rem(at_x + dx, 4) * 4 + lax.rem(at_z + dz, 4)
        return other, lax.rem(side + dl, 2)

    def same_core(offset):
        other, other_side = moved(offset)
        return (other, other_side * 2 + core)

    loads = [
        pltpu.make_async_copy(a, b, ld_sem.at[i])
        for i, (a, b) in enumerate((
            (coup_hbm, coup), (fmap_hbm, fmap), (src_hbm, src), (invd_hbm, invd), (wjac_hbm, wjac), (weight_hbm, weight), (ids_hbm, ids)))
    ]
    for copy in loads:
        copy.start()

    barrier = pltpu.get_barrier_semaphore()

    for offset in FAR_CHIPS:
        pl.semaphore_signal(barrier, inc=1, device_id=same_core(offset), device_id_type=MESH)
    for step in (1, 3):
        pl.semaphore_signal(barrier, inc=1, device_id=(blk, lax.rem(sub + step, NSUB)), device_id_type=MESH)

    loads[0].wait()
    loads[1].wait()
    for d in range(6):
        for u in range(NVAR):
            for v in range(NVAR):
                coef[d * 25 + u * 5 + v] = jnp.full((8, 128), coup[u, v, 0, d], jnp.float32)

    @pl.when(sub == 0)
    def _():
        for p in fields:
            p[:, 0] = jnp.zeros((NVAR, CK, CI), jnp.float32)

    @pl.when(sub == NSUB - 1)
    def _():
        for p in fields:
            p[:, CS + 1] = jnp.zeros((NVAR, CK, CI), jnp.float32)

    loads[2].wait()
    loads[3].wait()

    def first_row(s, packed):
        face, diag = list(packed[:NVAR]), list(packed[NVAR:])
        for v in range(NVAR):
            for t in range(KT):
                rows = slice(8 * t, 8 * t + 8)
                inv = invd[v, s, rows, :]
                value = inv * src[v, s, rows, :]
                p0[v, s + 1, rows, :] = value
                face[v] = place(lane1, value[:, 128:], 127, face_lane(0, t, s), face[v])
                face[v] = place(lane1, value[:, :128], 0, face_lane(1, t, s), face[v])
                diag[v] = place(lane1, inv[:, :128], 0, face_lane(0, t, s), diag[v])
                diag[v] = place(lane1, inv[:, 128:], 127, face_lane(1, t, s), diag[v])
        return tuple(face + diag)

    none = jnp.zeros((8, 128), jnp.float32)
    packed = lax.fori_loop(0, CS, first_row, (none,) * (2 * NVAR))
    face, diag = packed[:NVAR], packed[NVAR:]

    pl.semaphore_wait(barrier, 65)

    def up_copy(n, i):
        rows = pl.ds(*SPAN_ROWS[i])
        return pltpu.make_async_remote_copy(
            src_ref=fields[n].at[:, CS, rows], dst_ref=fields[n].at[:, 0, rows],
            send_sem=hs_sem.at[n, 0, i], recv_sem=hr_sem.at[n, 0, i],
            device_id=(blk, lax.rem(sub + 1, NSUB)), device_id_type=MESH)

    def down_copy(n, i):
        rows = pl.ds(*SPAN_ROWS[i])
        return pltpu.make_async_remote_copy(
            src_ref=fields[n].at[:, 1, rows], dst_ref=fields[n].at[:, CS + 1, rows],
            send_sem=hs_sem.at[n, 1, i], recv_sem=hr_sem.at[n, 1, i],
            device_id=(blk, lax.rem(sub + NSUB - 1, NSUB)), device_id_type=MESH)

    def start_spans(n):
        for i in range(2):
            pl.when(sub < NSUB - 1)(lambda: up_copy(n, i).start())
            pl.when(sub > 0)(lambda: down_copy(n, i).start())

    def spans_landed(n, i):
        pl.when(sub > 0)(lambda: up_copy(n, i).wait_recv())
        pl.when(sub < NSUB - 1)(lambda: down_copy(n, i).wait_recv())

    def send_faces(n):
        for v in range(NVAR):
            fsend[n, v] = face[v]
            fbufs[n][blk, v] = face[v]

        for offset in FAR_BLOCKS:
            pltpu.make_async_remote_copy(
                src_ref=fsend.at[n], dst_ref=fbufs[n].at[blk], send_sem=fs_sem.at[n], recv_sem=fr_sem.at[n],
                device_id=same_core(offset), device_id_type=MESH).start()

    def faces_landed(n):
        fbuf = fbufs[n]
        landed = fbuf.at[pl.ds(0, NBLK - 1)]
        pltpu.make_async_copy(landed, landed, fr_sem.at[n]).wait()
        low = fbuf[fmap[0, blk]]
        high = fbuf[fmap[1, blk]]
        from_low = lane1 < 64
        outer = [jnp.where(from_low, low[v], high[v]) for v in range(NVAR)]
        terms = []
        for u in range(NVAR):
            total = none
            for v in range(NVAR):
                total = total + jnp.where(from_low, coef[100 + u * 5 + v], coef[125 + u * 5 + v]) * outer[v]
            terms.append(diag[u] * total)
        return terms

    def add_faces(p, pad, s, terms, tiles=(0, KT)):
        for u in range(NVAR):
            for t in range(*tiles):
                rows = slice(8 * t, 8 * t + 8)
                low = place(lane1, terms[u], face_lane(0, t, s), 0, 0.0)
                high = place(lane1, terms[u], face_lane(1, t, s), 127, 0.0)
                p[u, s + pad, rows, 0:128] = p[u, s + pad, rows, 0:128] + low
                p[u, s + pad, rows, 128:256] = p[u, s + pad, rows, 128:256] + high

    def over(rows, step):
        lo, hi = rows
        lax.fori_loop(lo, hi, lambda s, c: (step(s), c)[1], 0)

    def ends(step):
        lax.fori_loop(0, 2, lambda i, c: (step(i * (CS - 1)), c)[1], 0)

    for n in range(SWEEPS - 1):
        p, q = fields[n], fields[n + 1]
        send_faces(n)
        if n > 0:
            ends(lambda s: add_faces(p, 1, s, extra))
        start_spans(n)
        if n > 0:
            over((1, CS - 1), lambda s: add_faces(p, 1, s, extra))
        step = lambda s, c: relax_row(s, p, q, 1, coef, src, invd, c)
        made = lax.fori_loop(1, CS - 1, step, (none,) * NVAR)
        spans_landed(n, 0)
        spans_landed(n, 1)
        made = lax.fori_loop(0, 2, lambda i, c: step(i * (CS - 1), c), made)
        extra = faces_landed(n)
        face = [made[u] + pltpu.roll(extra[u], 64, 1) for u in range(NVAR)]

    n = SWEEPS - 1
    p = fields[n]
    send_faces(n)
    ends(lambda s: add_faces(p, 1, s, extra))
    start_spans(n)
    over((1, CS - 1), lambda s: add_faces(p, 1, s, extra))

    def last_rows(s, first, end):
        relax_row(s, p, out, 0, coef, src, invd, (), first, end)

    over((1, CS - 1), lambda s: last_rows(s, 0, 1))
    over((1, 3), lambda s: last_rows(s, 1, KT))
    spans_landed(n, 0)
    ends(lambda s: last_rows(s, 0, 1))
    for copy in loads[4:]:
        copy.wait()

    def wall_of(c):
        total = jnp.zeros((CS, CI), jnp.float32)
        for v in range(NVAR):
            for k in range(2):
                total = total + wjac[c, v, k] * out[v, :, k, :]
        return total

    column = lax.broadcasted_iota(jnp.int32, (CS, CI), 1)
    inner = (column > 0) & (column < CI - 1)
    for c in range(3):
        wall[c] = jnp.where(inner, wall_of(c), 0.0)

    acc[...] = jnp.zeros_like(acc)

    def row_and_lane(point):
        high = point >> 7
        holder = (high * 171) >> 9
        order = (holder & 1) * 64 + (holder >> 1)
        return jnp.where(point < 0, -1, (high - 3 * holder) * 128 + order), point & 127

    def slots(step, carry):
        for i in range(2):
            m = 2 * step + i
            rank, low = row_and_lane(ids[m])
            pieces = []
            for c in range(3):
                value = weight[m] * wall[c]
                top = value.astype(jnp.bfloat16).astype(jnp.float32)
                pieces.append(top)
                pieces.append(value - top)
            for s in range(CS):
                lanes = slice((i * CS + s) * CI, (i * CS + s + 1) * CI)
                hit = lax.broadcasted_iota(jnp.int32, (384, CI), 0) == rank[s : s + 1, :]
                onehot[:, lanes] = jnp.where(hit, 1.0, 0.0).astype(jnp.bfloat16)
                match = lax.broadcasted_iota(jnp.int32, (128, CI), 0) == low[s : s + 1, :]
                for k in range(6):
                    spread[k * 128 : (k + 1) * 128, lanes] = jnp.where(match, pieces[k][s : s + 1, :], 0.0).astype(jnp.bfloat16)
        acc[...] = acc[...] + lax.dot_general(
            onehot[...], spread[...], (((1,), (1,)), ((), ())), preferred_element_type=jnp.float32)
        return carry

    lax.fori_loop(0, 4, slots, 0)

    extra = faces_landed(n)
    over((0, CS), lambda s: add_faces(out, 0, s, extra, (0, 1)))
    walls = [wall_of(c) for c in range(3)]
    marks = [jnp.full((8, 128), -1, jnp.int32), jnp.zeros((8, 128), jnp.int32)] + [none] * 3
    for m in range(8):
        rank, low = row_and_lane(ids[m])
        for i, x in enumerate([rank, low] + [weight[m] * walls[c] for c in range(3)]):
            marks[i] = place(lane1, x[:, :128], 0, 2 * m, marks[i])
            marks[i] = place(lane1, x[:, 128:], 127, 2 * m + 1, marks[i])
    line = lax.broadcasted_iota(jnp.int32, (1, 128), 1)
    flat = []
    for x in marks:
        total = x[0:1, :]
        for s in range(1, CS):
            total = jnp.where((line >> 4) == s, pltpu.roll(x[s : s + 1, :], 16 * s, 1), total)
        flat.append(total)
    hit = lax.broadcasted_iota(jnp.int32, (384, 128), 0) == flat[0]
    match = lax.broadcasted_iota(jnp.int32, (128, 128), 0) == flat[1]
    edge_spread = []
    for c in range(3):
        top = flat[2 + c].astype(jnp.bfloat16).astype(jnp.float32)
        for value in (top, flat[2 + c] - top):
            edge_spread.append(jnp.where(match, value, 0.0).astype(jnp.bfloat16))
    acc[...] = acc[...] + lax.dot_general(
        jnp.where(hit, 1.0, 0.0).astype(jnp.bfloat16), jnp.concatenate(edge_spread, 0), (((1,), (1,)), ((), ())),
        preferred_element_type=jnp.float32)
    for j in range(3):
        for c in range(3):
            for g in range(16):
                rows = slice(j * 128 + g * 8, j * 128 + g * 8 + 8)
                total = acc[rows, c * 256 : c * 256 + 128] + acc[rows, c * 256 + 128 : c * 256 + 256]
                dense[pl.ds(g * 128 + c * 3 + j, 8, stride=16), :] = total

    swap = pltpu.make_async_remote_copy(
        src_ref=dense.at[pl.ds((1 - core) * 1024, 1024)], dst_ref=pair, send_sem=sw_sem.at[0], recv_sem=sw_sem.at[1],
        device_id=(blk, side * 2 + 1 - core), device_id_type=MESH)
    swap.start()
    over((3, 5), lambda s: last_rows(s, 1, KT))
    swap.wait()

    def add(i, c):
        both = dense[pl.ds(core * 1024 + i * 16, 16), :] + pair[pl.ds(i * 16, 16), :]
        mine[i] = both[:9, :]
        return c

    lax.fori_loop(0, 64, add, 0, unroll=8)

    for d, offset in enumerate(FAR_CHIPS):
        other, other_side = moved(offset)
        pltpu.make_async_remote_copy(
            src_ref=mine.at[other * 2 + other_side], dst_ref=landing.at[d + 1], send_sem=ds_sem, recv_sem=dr_sem,
            device_id=same_core(offset), device_id_type=MESH).start()
    landing[0] = mine[chip]

    spans_landed(n, 1)
    over((5, CS - 1), lambda s: last_rows(s, 1, KT))
    ends(lambda s: last_rows(s, 1, KT))
    over((0, CS), lambda s: add_faces(out, 0, s, extra, (1, KT)))

    landed = landing.at[pl.ds(1, 63)]
    pltpu.make_async_copy(landed, landed, dr_sem).wait()
    total = lax.fori_loop(0, 64, lambda i, t: t + landing[i], jnp.zeros((9, 128), jnp.float32), unroll=8)
    for c in range(3):
        for j in range(3):
            sens[c : c + 1, j * 128 : (j + 1) * 128] = total[c * 3 + j : c * 3 + j + 1, :]
    pltpu.make_async_copy(landed, landed, ds_sem).wait()

    for n in range(SWEEPS):
        for i in range(2):
            pl.when(sub < NSUB - 1)(lambda: up_copy(n, i).wait_send())
            pl.when(sub > 0)(lambda: down_copy(n, i).wait_send())
        sent = fbufs[n].at[pl.ds(0, NBLK - 1)]
        pltpu.make_async_copy(sent, sent, fs_sem.at[n]).wait()


def body(source, inv_diag, coupling, face_map, wall_jac, ffd_weight, cp_ids):
    vmem = pl.BlockSpec(memory_space=pltpu.VMEM)
    hbm = pl.BlockSpec(memory_space=pltpu.HBM)
    f32, dma = jnp.float32, pltpu.SemaphoreType.DMA
    args = (jnp.transpose(coupling, (2, 3, 0, 1)), face_map.T, source, inv_diag, wall_jac, ffd_weight, cp_ids)
    face_buffer = pltpu.VMEM((NBLK, NVAR, 8, 128), f32)
    field = pltpu.VMEM((NVAR, CS + 2, CK, CI), f32)
    return pl.pallas_call(
        kernel,
        out_shape=(jax.ShapeDtypeStruct((NVAR, CS, CK, CI), f32), jax.ShapeDtypeStruct((3, 384), f32)),
        in_specs=[hbm] * 7,
        out_specs=(vmem, vmem),
        scratch_shapes=[
            pltpu.SMEM((NVAR, NVAR, 1, 6), f32),
            pltpu.SMEM((2, NBLK), jnp.int32),
            pltpu.VMEM((NVAR, CS, CK, CI), f32),
            pltpu.VMEM((NVAR, CS, CK, CI), f32),
            pltpu.VMEM((3, NVAR, 2, CS, CI), f32),
            pltpu.VMEM((8, CS, CI), f32),
            pltpu.VMEM((8, CS, CI), jnp.int32),
            pltpu.VMEM((150, 8, 128), f32),
            field,
            field,
            field,
            pltpu.VMEM((SWEEPS, NVAR, 8, 128), f32),
            face_buffer,
            face_buffer,
            face_buffer,
            pltpu.VMEM((3, CS, CI), f32),
            pltpu.VMEM((384, 2 * CS * CI), jnp.bfloat16),
            pltpu.VMEM((768, 2 * CS * CI), jnp.bfloat16),
            pltpu.VMEM((384, 768), f32),
            pltpu.VMEM((2048, 128), f32),
            pltpu.VMEM((1024, 128), f32),
            pltpu.VMEM((64, 9, 128), f32),
            pltpu.VMEM((64, 9, 128), f32),
            dma((7,)),
            dma((SWEEPS,)),
            dma((SWEEPS,)),
            dma((SWEEPS, 2, 2)),
            dma((SWEEPS, 2, 2)),
            dma((2,)),
            dma,
            dma,
        ],
        compiler_params=pltpu.CompilerParams(collective_id=0, has_side_effects=True, vmem_limit_bytes=44 << 20),
        name="adjoint",
    )(*[pltpu.with_memory_space_constraint(x, pltpu.HBM) for x in args])


def solution(mesh):
    in_specs = (
        P(None, "sub", None, "blk"),
        P(None, "sub", None, "blk"),
        P("blk", None, None, None),
        P(),
        P(None, None, None, "sub", "blk"),
        P(None, "sub", "blk"),
        P(None, "sub", "blk"),
    )
    out_specs = (P(None, "sub", None, "blk"), P(None, ("blk", "sub")))
    return jax.shard_map(body, mesh=mesh, in_specs=in_specs, out_specs=out_specs, check_vma=False)
```
